512 devices in a mesh: sec: 16 (over y, core), blk: 32 (over z, x).
Axes of the slice: x: 4, y: 8, z: 8, core: 2. Of those that a mesh axis runs over, the one named last changes fastest.
Arguments:
- left_built: bfloat16 [16, 6, 64, 256, 256], P('sec', None, 'blk'), may hold values from -0.375 to 0.375
- right_env: bfloat16 [16, 6, 64, 256, 256], P('sec', None, 'blk'), may hold values from -0.375 to 0.375
- psi_init: float32 [16, 64, 256, 256], P('sec', 'blk')
- block_dims: int32 [16, 64], P('sec', 'blk'), may hold values from 64 to 256, as said below
- ranks: int32 [16, 64], P('sec', 'blk'), may hold values from 2 to 128, as said below
- sketch: float32 [16, 64, 256, 128], P('sec', 'blk'), may hold values from -6 to 6
Outputs:
- truncated: float32 [16, 64, 256, 256], P('sec', 'blk')
- alphas: float32 [16, 4], P('sec')
- betas: float32 [16, 4], P('sec')
The draws below stay inside these ranges and needn't reach their ends.
Inputs may be any that keep to these rules, and one draw needn't show every extreme that they name: `block_dims`: in each section at least one block has dimension exactly 256. `ranks`: each rank is at most half of its block's dimension; in each section at least one block of dimension 256 has rank 256 // 2.
All inputs are finite; a program needn't handle non-finite values.
Results may differ from the reference program's by a relative error of at most 0.0096.
Values may be sent and summed in bfloat16 or wider, within the bound.
No kernel may reach another device: no remote copies, remote signals or barrier semaphores. Data moves between devices by JAX's collectives and lax.ppermute only.
A program may use at most 64 MiB of HBM per device.

```python
import jax
import jax.numpy as jnp
from jax import lax

B = 256
W = 6
NB = 2
STEPS = 4
RMAX = 128
SECTORS = 64
N_SEC = 16


def sector_table(key):
    keys = jax.random.split(jax.random.fold_in(key, 11), 3)
    dims = jax.random.randint(keys[0], (N_SEC, SECTORS), B // 4, B + 1)
    pick = jax.random.randint(keys[1], (N_SEC,), 0, SECTORS)
    hit = jnp.arange(SECTORS)[None, :] == pick[:, None]
    dims = jnp.where(hit, B, dims)
    ranks = jax.random.randint(keys[2], (N_SEC, SECTORS), 2, dims // 2 + 1)
    ranks = jnp.where(hit, B // 2, ranks)
    return (dims.astype(jnp.int32), ranks.astype(jnp.int32))


def draw_block_dims(key, part):
    return sector_table(key)[0]


def draw_ranks(key, part):
    return sector_table(key)[1]


def draw_psi_init(key, part):
    keys = jax.random.split(jax.random.fold_in(key, 23), 1)
    ramp = 3.0 ** (jnp.arange(SECTORS, dtype=jnp.float32) / max(SECTORS - 1, 1))
    ramp = ramp[None, :, None, None]
    base = jax.random.normal(keys[0], (N_SEC, SECTORS, B, B), jnp.float32)
    return (base * ramp).astype(jnp.float32)


def shard_levels(own_key, shape, shards, low, largest):
    level, own = 1.0, jax.random.fold_in(own_key, 6)
    for dim, shards_of in shards:
        draws = jnp.exp(jax.random.uniform(jax.random.fold_in(own, dim), (shards_of,), jnp.float32, low / len(shards), largest / len(shards)))
        level = level * jnp.repeat(draws, shape[dim] // shards_of).reshape([-1 if axis == dim else 1 for axis in range(len(shape))])
    return level


def noise(key, shape, spread, limit, cuts=(), kind=jnp.bfloat16):
    level = shard_levels(key, shape, cuts, -0.22, 0.18) if cuts else 1.0
    result = jax.random.normal(key, shape, jnp.float32) * spread * level
    return jnp.minimum(jnp.maximum(result, -limit), limit).astype(kind)


def setup_inputs(seed: int = 0) -> dict:
    seeds = jax.random.split(jax.random.key(seed), 7)
    left_built = noise(seeds[0], (N_SEC, W, SECTORS, B, B), B ** -0.5, 0.375, ((0, 16), (2, 32)))
    right_env = noise(seeds[1], (N_SEC, W, SECTORS, B, B), B ** -0.5, 0.375, ((0, 16), (2, 32)))
    psi_init = draw_psi_init(jax.random.fold_in(seeds[6], 71), 0)
    block_dims = draw_block_dims(jax.random.fold_in(seeds[6], 71), 0)
    ranks = draw_ranks(jax.random.fold_in(seeds[6], 71), 0)
    sketch = noise(seeds[5], (N_SEC, SECTORS, B, RMAX), 1.0, 6.0, ((0, 16), (1, 32)), jnp.float32)
    return dict(left_built=left_built, right_env=right_env, psi_init=psi_init, block_dims=block_dims, ranks=ranks, sketch=sketch)


def apply_ham(vbf, left, right, cellmask, spin_low, spin_high):
    vals = lax.optimization_barrier(vbf).astype(jnp.float32)
    width = NB + 1
    padded = jnp.pad(vals, ((width, width), (0, 0), (0, 0)))
    sources = [vals, vals, padded[1:1 + SECTORS], padded[2 * NB + 1:2 * NB + 1 + SECTORS], padded[0:SECTORS] * spin_low, padded[2 * NB + 2:2 * NB + 2 + SECTORS] * spin_high]
    total = jnp.zeros(vals.shape, jnp.float32)
    for k in range(W):
        mixed = jnp.einsum('qab,qcb->qac', sources[k], right[k].astype(jnp.float32))
        mixed = lax.optimization_barrier(mixed.astype(jnp.bfloat16)).astype(jnp.float32)
        total = total + jnp.einsum('qab,qbc->qac', left[k].astype(jnp.float32), mixed)
    return total * cellmask

def project_block(blockv, sketchb, cmask):
    hp = lax.Precision.HIGHEST
    ymat = jnp.dot(blockv, sketchb, precision=hp) * cmask[None, :]
    gram = jnp.dot(ymat.T, ymat, precision=hp) + jnp.diag(1.0 - cmask)
    factor = jnp.linalg.cholesky(gram)
    rhs = jnp.dot(ymat.T, blockv, precision=hp)
    inner = lax.linalg.triangular_solve(factor, rhs, left_side=True, lower=True)
    coef = lax.linalg.triangular_solve(factor, inner, left_side=True, lower=True, transpose_a=True)
    return jnp.dot(ymat, coef, precision=hp)

def one_section(inputs):
    left, right, start, dims, rank_row, sketch_sec = inputs
    iota = jnp.arange(B)
    rowmask = (iota[None, :] < dims[:, None]).astype(jnp.float32)
    cellmask = rowmask[:, :, None] * rowmask[:, None, :]
    spin = jnp.arange(SECTORS) % NB
    spin_low = (spin >= 1).astype(jnp.float32)[:, None, None]
    spin_high = (spin <= NB - 2).astype(jnp.float32)[:, None, None]
    count = float(SECTORS * B * B)
    vec = start * cellmask
    vec = vec * jnp.sqrt(count / jnp.sum(vec * vec))
    prev = jnp.zeros_like(vec)
    beta = jnp.float32(0.0)
    alpha_list = []
    beta_list = []
    for step in range(STEPS):
        image = apply_ham(vec.astype(jnp.bfloat16), left, right, cellmask, spin_low, spin_high)
        alpha = jnp.sum(vec * image) / count
        resid = image - alpha * vec - beta * prev
        beta = jnp.sqrt(jnp.sum(resid * resid) / count + 1e-06)
        prev = vec
        vec = resid / beta
        alpha_list.append(alpha)
        beta_list.append(beta)
    cmask = (jnp.arange(B // 2)[None, :] < rank_row[:, None]).astype(jnp.float32)
    cut_off = jax.vmap(project_block)(vec, sketch_sec, cmask)
    return (cut_off, jnp.stack(alpha_list), jnp.stack(beta_list))

def reference(left_built, right_env, psi_init, block_dims, ranks, sketch):
    left_all = jnp.roll(left_built, 1, axis=0)
    return lax.map(one_section, (left_all, right_env, psi_init, block_dims, ranks, sketch))
```

```python
import functools

import jax
import jax.numpy as jnp
from jax import lax
from jax.experimental import pallas as pl
from jax.experimental.pallas import tpu as pltpu
from jax.sharding import PartitionSpec as P

STEPS = 4
F32 = jnp.float32
BF16 = jnp.bfloat16
VM = pl.BlockSpec(memory_space=pltpu.VMEM)
SM = pl.BlockSpec(memory_space=pltpu.SMEM)


def total(x):
    return jnp.sum(jnp.sum(x, axis=0, keepdims=True), axis=1, keepdims=True)


def dot_nt(a, b):
    return lax.dot_general(a, b, (((1,), (1,)), ((), ())), preferred_element_type=F32)


def dot_nn(a, b):
    return jnp.dot(a, b, preferred_element_type=F32)


def cell_mask(dims, q, side):
    rows = lax.broadcasted_iota(jnp.int32, (side, side), 0)
    cols = lax.broadcasted_iota(jnp.int32, (side, side), 1)
    return jnp.logical_and(rows < dims[q], cols < dims[q])


def lay_rows(values, shape):
    lane = lax.broadcasted_iota(jnp.int32, shape, 1)
    out = jnp.zeros(shape, F32)
    for k, value in enumerate(values):
        out = jnp.where(lane == k, value, out)
    return out


def read_rows(gathered, k):
    return jnp.broadcast_to(gathered[:, k : k + 1], gathered.shape)


def coefficients(gathered, count, places):
    alpha = jnp.sum(read_rows(gathered, 0), axis=0, keepdims=True) / count
    dev = read_rows(gathered, 3) - alpha
    parts = (
        read_rows(gathered, 1)
        + 2.0 * dev * read_rows(gathered, 4)
        + dev * read_rows(gathered, 2) * dev
    )
    resid_sq = jnp.maximum(jnp.sum(parts, axis=0, keepdims=True), 0.0)
    beta = jnp.sqrt(resid_sq / count + 1e-06)
    row = lax.broadcasted_iota(jnp.int32, gathered.shape, 0)
    found = [
        jnp.sum(jnp.where(row == place, dev, 0.0), axis=0, keepdims=True)[:, :1]
        for place in places
    ]
    return alpha, beta, found


def record(acc, step, alpha, beta):
    lane = lax.broadcasted_iota(jnp.int32, acc.shape, 1)
    row = lax.broadcasted_iota(jnp.int32, acc.shape, 0)
    here = lane == step
    acc = jnp.where(jnp.logical_and(here, row == 0), alpha, acc)
    return jnp.where(jnp.logical_and(here, row == 1), beta, acc)


def begin_kernel(dims, psi, masked, sent, sums):
    blocks, side = psi.shape[0], psi.shape[1]
    square = jnp.zeros((1, 1), F32)
    for q in range(blocks):
        x = jnp.where(cell_mask(dims, q, side), psi[q], 0.0)
        masked[q] = x
        sent[q] = x.astype(BF16)
        square = square + total(x * x)
    sums[...] = jnp.broadcast_to(square, sums.shape)


def step_kernel(step, count, place, dims, gathered, acc, left, right, held, lower, upper, *rest):
    if step == 0:
        sent, now, vec, mixes, sums, acc_out = rest
    else:
        before, mixed_before, sent, now, vec, mixes, sums, acc_out = rest
    blocks, side = held.shape[0], held.shape[1]
    me = place[0]
    if step == 0:
        start_sq = jnp.sum(read_rows(gathered, 0), axis=0, keepdims=True)
        inv = jnp.sqrt(count / start_sq)[:, :1]
        acc_out[...] = jnp.zeros(acc_out.shape, F32)
    else:
        alpha, beta, (d_own, d_low, d_up) = coefficients(
            gathered[...], count, (me, me - 1, me + 1)
        )
        acc_out[...] = record(acc[...], step - 1, alpha, beta)
        beta = beta[:, :1]
        inv = 1.0 / beta
    corr = jnp.zeros((1, 1), F32)
    norm = jnp.zeros((1, 1), F32)
    image_dot = jnp.zeros((1, 1), F32)

    def mixed_from(slot, block, k, q, dev):
        mixed = dot_nt(block, right[k, q])
        if step > 0:
            mixed = mixed + dev * mixed_before[slot]
        mixed = mixed * inv
        mixes[slot] = mixed
        return mixed.astype(BF16)

    for q in range(blocks):
        if step == 0:
            v = held[q] * inv
            low = up = None
        else:
            v = (held[q] + d_own * before[q]) * inv
            low, up = d_low, d_up
        vec[q] = v
        x = v.astype(BF16)
        sums_q = dot_nn(left[0, q], dot_nt(x, right[0, q]).astype(BF16))
        sums_q += dot_nn(left[1, q], dot_nt(x, right[1, q]).astype(BF16))
        sums_q += dot_nn(left[2, q], mixed_from(q, lower[q], 2, q, low))
        sums_q += dot_nn(left[3, q], mixed_from(2 + q, upper[q], 3, q, up))
        if q == 1:
            sums_q += dot_nn(left[4, q], mixed_from(4, lower[0], 4, q, low))
        else:
            sums_q += dot_nn(left[5, q], mixed_from(5, upper[1], 5, q, up))
        w = jnp.where(cell_mask(dims, q, side), sums_q, 0.0)
        corr = corr + total(v * w)
        norm = norm + total(v * v)
        if step > 0:
            w = w - beta * before[q]
            image_dot = image_dot + total(v * w)
        now[q] = w
    if step == 0:
        image_dot = corr
    near = jnp.where(norm > 1e-12, image_dot / jnp.maximum(norm, 1e-12), 0.0)
    square = jnp.zeros((1, 1), F32)
    cross = jnp.zeros((1, 1), F32)
    for q in range(blocks):
        t = now[q] - near * vec[q]
        now[q] = t
        sent[q] = t.astype(BF16)
        square = square + total(t * t)
        cross = cross + total(t * vec[q])
    sums[...] = lay_rows((corr, square, norm, near, cross), sums.shape)


def finish_kernel(step, count, place, gathered, acc, held, before, out, acc_out):
    alpha, beta, (d_own,) = coefficients(gathered[...], count, (place[0],))
    acc_out[...] = record(acc[...], step, alpha, beta)
    inv = 1.0 / beta[:, :1]
    for q in range(held.shape[0]):
        out[q] = (held[q] + d_own * before[q]) * inv


def project_block(blockv, sketchb, cmask):
    hp = lax.Precision.HIGHEST
    ymat = jnp.dot(blockv, sketchb, precision=hp) * cmask[None, :]
    gram = jnp.dot(ymat.T, ymat, precision=hp) + jnp.diag(1.0 - cmask)
    factor = jnp.linalg.cholesky(gram)
    rhs = jnp.dot(ymat.T, blockv, precision=hp)
    inner = lax.linalg.triangular_solve(factor, rhs, left_side=True, lower=True)
    coef = lax.linalg.triangular_solve(factor, inner, left_side=True, lower=True, transpose_a=True)
    return jnp.dot(ymat, coef, precision=hp)


def shards(left_built, right_env, psi_init, block_dims, ranks, sketch):
    _, blocks, side, _ = psi_init.shape
    near = lax.axis_size("blk")
    count = float(near * blocks * side * side)
    secs = lax.axis_size("sec")
    left = lax.ppermute(left_built[0], "sec", [(i, (i + 1) % secs) for i in range(secs)])
    right = right_env[0]
    dims = block_dims[0]
    place = lax.axis_index("blk").astype(jnp.int32).reshape(1)
    block_f32 = jax.ShapeDtypeStruct((blocks, side, side), F32)
    block_bf16 = jax.ShapeDtypeStruct((blocks, side, side), BF16)
    rows = jax.ShapeDtypeStruct((near, 128), F32)
    small = jax.ShapeDtypeStruct((8, 128), F32)
    mixes = jax.ShapeDtypeStruct((6, side, side), F32)

    def halo(block):
        low = lax.ppermute(block, "blk", [(i, i + 1) for i in range(near - 1)])
        up = lax.ppermute(block, "blk", [(i + 1, i) for i in range(near - 1)])
        return low, up

    def everyone(sums):
        return lax.all_to_all(sums, "blk", 0, 0, tiled=True)

    held, sent, sums = pl.pallas_call(
        begin_kernel,
        out_shape=(block_f32, block_bf16, rows),
        in_specs=[SM, VM],
        out_specs=(VM, VM, VM),
        name="begin",
    )(dims, psi_init[0])
    acc = jnp.zeros((8, 128), F32)
    extra = ()
    for step in range(STEPS):
        low, up = halo(sent)
        gathered = everyone(sums)
        ins = (place, dims, gathered, acc, left, right, held, low, up) + extra
        sent, held, vec, mixed, sums, acc = pl.pallas_call(
            functools.partial(step_kernel, step, count),
            out_shape=(block_bf16, block_f32, block_f32, mixes, rows, small),
            in_specs=[SM, SM] + [VM] * (len(ins) - 2),
            out_specs=(VM,) * 6,
            name="step%d" % step,
        )(*ins)
        extra = (vec, mixed)
    gathered = everyone(sums)
    last, acc = pl.pallas_call(
        functools.partial(finish_kernel, STEPS - 1, count),
        out_shape=(block_f32, small),
        in_specs=[SM] + [VM] * 4,
        out_specs=(VM, VM),
        name="finish",
    )(place, gathered, acc, held, extra[0])
    rmax = sketch.shape[3]
    cmask = (jnp.arange(rmax)[None, :] < ranks[0][:, None]).astype(F32)
    truncated = jax.vmap(project_block)(last, sketch[0], cmask)
    return (truncated[None], acc[0:1, :STEPS], acc[1:2, :STEPS])


def solution(mesh):
    placed = (
        P("sec", None, "blk", None, None),
        P("sec", None, "blk", None, None),
        P("sec", "blk", None, None),
        P("sec", "blk"),
        P("sec", "blk"),
        P("sec", "blk", None, None),
    )
    return jax.shard_map(
        shards,
        mesh=mesh,
        in_specs=placed,
        out_specs=(P("sec", "blk", None, None), P("sec", None), P("sec", None)),
        check_vma=False,
    )
```

```python
import functools

import jax
import jax.numpy as jnp
from jax import lax
from jax.experimental import pallas as pl
from jax.experimental.pallas import tpu as pltpu
from jax.sharding import PartitionSpec as P

STEPS = 4
PANEL = 32
F32 = jnp.float32
BF16 = jnp.bfloat16
VM = pl.BlockSpec(memory_space=pltpu.VMEM)
SM = pl.BlockSpec(memory_space=pltpu.SMEM)


def total(x):
    return jnp.sum(jnp.sum(x, axis=0, keepdims=True), axis=1, keepdims=True)


def dot_nt(a, b):
    return lax.dot_general(a, b, (((1,), (1,)), ((), ())), preferred_element_type=F32)


def dot_nn(a, b):
    return jnp.dot(a, b, preferred_element_type=F32)


def cell_mask(dims, q, side):
    rows = lax.broadcasted_iota(jnp.int32, (side, side), 0)
    cols = lax.broadcasted_iota(jnp.int32, (side, side), 1)
    return jnp.logical_and(rows < dims[q], cols < dims[q])


def lay_rows(values, shape):
    lane = lax.broadcasted_iota(jnp.int32, shape, 1)
    out = jnp.zeros(shape, F32)
    for k, value in enumerate(values):
        out = jnp.where(lane == k, value, out)
    return out


def read_rows(gathered, k):
    return jnp.broadcast_to(gathered[:, k : k + 1], gathered.shape)


def coefficients(gathered, count, places):
    alpha = jnp.sum(read_rows(gathered, 0), axis=0, keepdims=True) / count
    dev = read_rows(gathered, 3) - alpha
    parts = (
        read_rows(gathered, 1)
        + 2.0 * dev * read_rows(gathered, 4)
        + dev * read_rows(gathered, 2) * dev
    )
    resid_sq = jnp.maximum(jnp.sum(parts, axis=0, keepdims=True), 0.0)
    beta = jnp.sqrt(resid_sq / count + 1e-06)
    row = lax.broadcasted_iota(jnp.int32, gathered.shape, 0)
    found = [
        jnp.sum(jnp.where(row == place, dev, 0.0), axis=0, keepdims=True)[:, :1]
        for place in places
    ]
    return alpha, beta, found


def record(acc, step, alpha, beta):
    lane = lax.broadcasted_iota(jnp.int32, acc.shape, 1)
    row = lax.broadcasted_iota(jnp.int32, acc.shape, 0)
    here = lane == step
    acc = jnp.where(jnp.logical_and(here, row == 0), alpha, acc)
    return jnp.where(jnp.logical_and(here, row == 1), beta, acc)


def begin_kernel(dims, psi, masked, sent, sums):
    blocks, side = psi.shape[0], psi.shape[1]
    square = jnp.zeros((1, 1), F32)
    for q in range(blocks):
        x = jnp.where(cell_mask(dims, q, side), psi[q], 0.0)
        masked[q] = x
        sent[q] = x.astype(BF16)
        square = square + total(x * x)
    sums[...] = jnp.broadcast_to(square, sums.shape)


def step_kernel(step, count, place, dims, gathered, acc, left, right, held, lower, upper, *rest):
    if step == 0:
        sent, now, vec, mixes, sums, acc_out = rest
    else:
        before, mixed_before, sent, now, vec, mixes, sums, acc_out = rest
    blocks, side = held.shape[0], held.shape[1]
    me = place[0]
    if step == 0:
        start_sq = jnp.sum(read_rows(gathered, 0), axis=0, keepdims=True)
        inv = jnp.sqrt(count / start_sq)[:, :1]
        acc_out[...] = jnp.zeros(acc_out.shape, F32)
    else:
        alpha, beta, (d_own, d_low, d_up) = coefficients(
            gathered[...], count, (me, me - 1, me + 1)
        )
        acc_out[...] = record(acc[...], step - 1, alpha, beta)
        beta = beta[:, :1]
        inv = 1.0 / beta
    corr = jnp.zeros((1, 1), F32)
    norm = jnp.zeros((1, 1), F32)
    image_dot = jnp.zeros((1, 1), F32)

    def mixed_from(slot, block, k, q, dev):
        mixed = dot_nt(block, right[k, q])
        if step > 0:
            mixed = mixed + dev * mixed_before[slot]
        mixed = mixed * inv
        mixes[slot] = mixed
        return mixed.astype(BF16)

    for q in range(blocks):
        if step == 0:
            v = held[q] * inv
            low = up = None
        else:
            v = (held[q] + d_own * before[q]) * inv
            low, up = d_low, d_up
        vec[q] = v
        x = v.astype(BF16)
        sums_q = dot_nn(left[0, q], dot_nt(x, right[0, q]).astype(BF16))
        sums_q += dot_nn(left[1, q], dot_nt(x, right[1, q]).astype(BF16))
        sums_q += dot_nn(left[2, q], mixed_from(q, lower[q], 2, q, low))
        sums_q += dot_nn(left[3, q], mixed_from(2 + q, upper[q], 3, q, up))
        if q == 1:
            sums_q += dot_nn(left[4, q], mixed_from(4, lower[0], 4, q, low))
        else:
            sums_q += dot_nn(left[5, q], mixed_from(5, upper[1], 5, q, up))
        w = jnp.where(cell_mask(dims, q, side), sums_q, 0.0)
        corr = corr + total(v * w)
        norm = norm + total(v * v)
        if step > 0:
            w = w - beta * before[q]
            image_dot = image_dot + total(v * w)
        now[q] = w
    if step == 0:
        image_dot = corr
    near = jnp.where(norm > 1e-12, image_dot / jnp.maximum(norm, 1e-12), 0.0)
    square = jnp.zeros((1, 1), F32)
    cross = jnp.zeros((1, 1), F32)
    for q in range(blocks):
        t = now[q] - near * vec[q]
        now[q] = t
        sent[q] = t.astype(BF16)
        square = square + total(t * t)
        cross = cross + total(t * vec[q])
    sums[...] = lay_rows((corr, square, norm, near, cross), sums.shape)


def dot_hp(a, b, dims):
    return lax.dot_general(a, b, (dims, ((), ())), precision=lax.Precision.HIGHEST, preferred_element_type=F32)

def panel_inverse(blocks, b):
    lane = lax.broadcasted_iota(jnp.int32, (8, 128), 1)
    row = lax.broadcasted_iota(jnp.int32, (8, 128), 0)
    first = lane < 64
    tiles = b // 8
    def column(k, r):
        one, two = (jnp.broadcast_to(x[8*r:8*r+8, k:k+1], (8, 128)) for x in blocks)
        return jnp.where(first, one, two)
    cols = [[column(k, r) for r in range(tiles)] for k in range(b)]
    own = jnp.where(first, lane, lane - 64)
    inv = [jnp.where(own == row + 8 * r, 1.0, 0.0).astype(F32) for r in range(tiles)]
    diag = [jnp.ones((8, 128), F32) for r in range(tiles)]
    for j in range(b):
        t, s = divmod(j, 8)
        pivot = jnp.broadcast_to(cols[j][t][s:s+1], (8, 128))
        diag[t] = jnp.where(row == s, pivot, diag[t])
        over = 1.0 / pivot
        inv_row = jnp.broadcast_to(inv[t][s:s+1], (8, 128))
        rows = [jnp.broadcast_to(cols[k][t][s:s+1], (8, 128)) for k in range(j + 1, b)]
        for r in range((j + 1) // 8, tiles):
            m = cols[j][r] * over
            if r == t:
                m = jnp.where(row > s, m, 0.0)
            for k in range(j + 1, b):
                cols[k][r] = cols[k][r] - m * rows[k - j - 1]
            inv[r] = inv[r] - m * inv_row
    full = jnp.concatenate([inv[r] * lax.rsqrt(diag[r]) for r in range(tiles)], axis=0)
    return full[:, :b], full[:, 64:64 + b]

def inverse_factors(work, b):
    n = work.shape[1]
    lane = lax.broadcasted_iota(jnp.int32, (b, n), 1)
    row = lax.broadcasted_iota(jnp.int32, (b, n), 0)
    for lo in range(0, n, b):
        hi = lo + b
        inv = panel_inverse([work[q, lo:hi, lo:hi] for q in range(2)], b)
        inside = jnp.logical_and(lane >= lo, lane < hi)
        unit = jnp.where(lane == row + lo, 1.0, 0.0)
        for q in range(2):
            panel = jnp.where(inside, unit, work[q, lo:hi, :])
            panel = dot_hp(inv[q], panel, ((1,), (0,)))
            work[q, lo:hi, :] = panel
            if hi < n:
                rest = work[q, hi:n, :]
                tail_lane = lax.broadcasted_iota(jnp.int32, rest.shape, 1)
                rest = jnp.where(jnp.logical_and(tail_lane >= lo, tail_lane < hi), 0.0, rest)
                work[q, hi:n, :] = rest - dot_hp(panel[:, hi:n], panel, ((0,), (0,)))

def truncate(ranks, sketch, vec, out, work, tall, rhs):
    n = sketch.shape[2]
    lane = lax.broadcasted_iota(jnp.int32, (1, n), 1)
    rows = lax.broadcasted_iota(jnp.int32, (n, n), 0)
    cols = lax.broadcasted_iota(jnp.int32, (n, n), 1)
    for q in range(2):
        y = dot_hp(vec[q], sketch[q], ((1,), (0,)))
        y = jnp.where(lane < ranks[q], y, 0.0)
        tall[q] = y
        spare = jnp.where(jnp.logical_and(rows == cols, cols >= ranks[q]), 1.0, 0.0)
        work[q] = dot_hp(y, y, ((0,), (0,))) + spare
    inverse_factors(work, PANEL)
    for q in range(2):
        rhs[q] = dot_hp(tall[q], vec[q], ((0,), (0,)))
        factor = jnp.where(rows >= cols, work[q], 0.0)
        inner = dot_hp(factor, rhs[q], ((1,), (0,)))
        coef = dot_hp(factor, inner, ((0,), (0,)))
        out[q] = dot_hp(tall[q], coef, ((1,), (0,)))


def finish_kernel(step, count, place, ranks, gathered, acc, held, before, sketch, out, acc_out, vec, work, tall, rhs):
    alpha, beta, (d_own,) = coefficients(gathered[...], count, (place[0],))
    acc_out[...] = record(acc[...], step, alpha, beta)
    inv = 1.0 / beta[:, :1]
    for q in range(held.shape[0]):
        vec[q] = (held[q] + d_own * before[q]) * inv
    truncate(ranks, sketch, vec, out, work, tall, rhs)


def keep(x):
    return pltpu.with_memory_space_constraint(x, pltpu.VMEM)


def shards(left_built, right_env, psi_init, block_dims, ranks, sketch):
    _, blocks, side, _ = psi_init.shape
    near = lax.axis_size("blk")
    count = float(near * blocks * side * side)
    secs = lax.axis_size("sec")
    left = lax.ppermute(left_built[0], "sec", [(i, (i + 1) % secs) for i in range(secs)])
    right = right_env[0]
    dims = block_dims[0]
    place = lax.axis_index("blk").astype(jnp.int32).reshape(1)
    block_f32 = jax.ShapeDtypeStruct((blocks, side, side), F32)
    block_bf16 = pltpu.VMEM((blocks, side, side), BF16)
    rows = pltpu.VMEM((near, 128), F32)
    small = pltpu.VMEM((8, 128), F32)
    mixes = jax.ShapeDtypeStruct((6, side, side), F32)

    def halo(block):
        low = lax.ppermute(block, "blk", [(i, i + 1) for i in range(near - 1)])
        up = lax.ppermute(block, "blk", [(i + 1, i) for i in range(near - 1)])
        return low, up

    def everyone(sums):
        return lax.all_to_all(sums, "blk", 0, 0, tiled=True)

    held, sent, sums = pl.pallas_call(
        begin_kernel,
        out_shape=(block_f32, block_bf16, rows),
        in_specs=[SM, VM],
        out_specs=(VM, VM, VM),
        name="begin",
    )(dims, psi_init[0])
    acc = jnp.zeros((8, 128), F32)
    extra = ()
    for step in range(STEPS):
        low, up = halo(sent)
        gathered = everyone(sums)
        ins = (place, dims, keep(gathered), acc, left, right, held, keep(low), keep(up)) + extra
        sent, held, vec, mixed, sums, acc = pl.pallas_call(
            functools.partial(step_kernel, step, count),
            out_shape=(block_bf16, block_f32, block_f32, mixes, rows, small),
            in_specs=[SM, SM] + [VM] * (len(ins) - 2),
            out_specs=(VM,) * 6,
            name="step%d" % step,
        )(*ins)
        extra = (vec, mixed)
    gathered = everyone(sums)
    rmax = sketch.shape[3]
    truncated, acc = pl.pallas_call(
        functools.partial(finish_kernel, STEPS - 1, count),
        out_shape=(jax.ShapeDtypeStruct((blocks, side, side), F32), small),
        in_specs=[SM, SM] + [VM] * 5,
        out_specs=(VM, VM),
        scratch_shapes=[
            pltpu.VMEM((blocks, side, side), F32),
            pltpu.VMEM((blocks, rmax, rmax), F32),
            pltpu.VMEM((blocks, side, rmax), F32),
            pltpu.VMEM((blocks, rmax, side), F32),
        ],
        name="finish",
    )(place, ranks[0], keep(gathered), acc, held, extra[0], sketch[0])
    return (truncated[None], acc[0:1, :STEPS], acc[1:2, :STEPS])


def solution(mesh):
    placed = (
        P("sec", None, "blk", None, None),
        P("sec", None, "blk", None, None),
        P("sec", "blk", None, None),
        P("sec", "blk"),
        P("sec", "blk"),
        P("sec", "blk", None, None),
    )
    return jax.shard_map(
        shards,
        mesh=mesh,
        in_specs=placed,
        out_specs=(P("sec", "blk", None, None), P("sec", None), P("sec", None)),
        check_vma=False,
    )
```

```python
import functools

import jax
import jax.numpy as jnp
from jax import lax
from jax.experimental import pallas as pl
from jax.experimental.pallas import tpu as pltpu
from jax.sharding import PartitionSpec as P

STEPS = 4
PANEL = 32
F32 = jnp.float32
BF16 = jnp.bfloat16
VM = pl.BlockSpec(memory_space=pltpu.VMEM)
SM = pl.BlockSpec(memory_space=pltpu.SMEM)
AN = pl.BlockSpec(memory_space=pl.ANY)


def total(x):
    return jnp.sum(jnp.sum(x, axis=0, keepdims=True), axis=1, keepdims=True)


def dot_nt(a, b):
    return lax.dot_general(a, b, (((1,), (1,)), ((), ())), preferred_element_type=F32)


def dot_nn(a, b):
    return jnp.dot(a, b, preferred_element_type=F32)


def cell_mask(dims, q, side):
    rows = lax.broadcasted_iota(jnp.int32, (side, side), 0)
    cols = lax.broadcasted_iota(jnp.int32, (side, side), 1)
    return jnp.logical_and(rows < dims[q], cols < dims[q])


def lay_rows(values, shape):
    lane = lax.broadcasted_iota(jnp.int32, shape, 1)
    out = jnp.zeros(shape, F32)
    for k, value in values.items():
        out = jnp.where(lane == k, value, out)
    return out


def read_rows(gathered, k):
    return jnp.broadcast_to(gathered[:, k : k + 1], gathered.shape)


D, S, V, A, C, PV, PT, EE, EV, ET, UV, UT, UU, EU, BETA = range(15)


def pair_coefficients(gathered, count, second, places):
    get = lambda k: read_rows(gathered, k)
    over = lambda x: jnp.sum(x, axis=0, keepdims=True)
    tt, vv, near, tv = get(S), get(V), get(A), get(C)
    pv, pt, ev, et = get(PV), get(PT), get(EV), get(ET)
    alpha = over(get(D)) / count
    dev = near - alpha
    resid = jnp.maximum(over(tt + 2.0 * dev * tv + dev * vv * dev), 0.0)
    beta = jnp.sqrt(resid / count + 1e-06)
    qt, qv = pt + dev, pv + dev * near
    inner = et + qt * tt + qv * tv + dev * (ev + qt * tv + qv * vv)
    if second:
        uv, ut, uu, eu = get(UV), get(UT), get(UU), get(EU)
        gu = dev * get(BETA)
        inner = inner + gu * ut + dev * (gu * uv)
    beta_sq = beta * beta
    alpha2 = over(inner) / (beta_sq * count)
    gt = qt - alpha2
    gv = qv - alpha2 * dev - beta_sq
    parts = get(EE) + gt * tt * gt + gv * vv * gv + 2.0 * (gt * et + gv * ev + gv * gt * tv)
    if second:
        parts = parts + gu * uu * gu + 2.0 * gu * (eu + gt * ut + gv * uv)
    resid2 = jnp.maximum(over(parts), 0.0)
    beta2 = jnp.sqrt(resid2 / (beta_sq * count) + 1e-06)
    row = lax.broadcasted_iota(jnp.int32, gathered.shape, 0)
    weights = [dev, gt, gv] + ([gu] if second else [])
    found = [
        [over(jnp.where(row == place, x, 0.0))[:, :1] for x in weights] for place in places
    ]
    return (alpha, beta, alpha2, beta2), found


def record(acc, step, alpha, beta):
    lane = lax.broadcasted_iota(jnp.int32, acc.shape, 1)
    row = lax.broadcasted_iota(jnp.int32, acc.shape, 0)
    here = lane == step
    acc = jnp.where(jnp.logical_and(here, row == 0), alpha, acc)
    return jnp.where(jnp.logical_and(here, row == 1), beta, acc)


def begin_kernel(dims, psi, masked, sent, sums):
    blocks, side = psi.shape[0], psi.shape[1]
    square = jnp.zeros((1, 1), F32)
    for q in range(blocks):
        x = jnp.where(cell_mask(dims, q, side), psi[q], 0.0)
        masked[q] = x
        sent[q * side : (q + 1) * side, :] = x.astype(BF16)
        square = square + total(x * x)
    sums[...] = jnp.broadcast_to(square, sums.shape)


NEAR = (
    (0, 0, 0, 2, 0),
    (1, 0, 1, 2, 1),
    (2, 1, 0, 3, 0),
    (3, 1, 1, 3, 1),
    (4, 0, 0, 4, 1),
    (5, 1, 1, 5, 0),
)


def from_lower(left, mixed, q):
    part = dot_nn(left[2, q], mixed[q])
    return part + dot_nn(left[4, q], mixed[4]) if q == 1 else part


def from_upper(left, mixed, q):
    part = dot_nn(left[3, q], mixed[2 + q])
    return part + dot_nn(left[5, q], mixed[5]) if q == 0 else part


def from_own(left, right, x, q):
    one = dot_nn(left[0, q], dot_nt(x, right[0, q]).astype(BF16))
    return one + dot_nn(left[1, q], dot_nt(x, right[1, q]).astype(BF16))


def ratio(top, bottom):
    return jnp.where(bottom > 1e-12, top / jnp.maximum(bottom, 1e-12), 0.0)


def three_parts(x):
    high = x.astype(BF16)
    rest = x - high.astype(F32)
    middle = rest.astype(BF16)
    return high, middle, (rest - middle.astype(F32)).astype(BF16)


def first_kernel(second, count, side, place, dims, gathered, acc, left_in, right_in, lower, upper, *rest):
    if second:
        resid, held, before, mixed_t, mixed_v = rest[:5]
        sent, now, vec, low_part, up_part, own_sums, acc_out, old = rest[5:13]
        left, right, mixes, mixed_tt, mixed_vv, sems = rest[13:]
    else:
        start = rest[0]
        sent, now, vec, low_part, up_part, own_sums, mixes_out = rest[1:8]
        left, right, mixes, sems = rest[8:]
    copies = [pltpu.make_async_copy(right_in, right, sems.at[0])]
    if second:
        copies.append(pltpu.make_async_copy(mixed_t, mixed_tt, sems.at[2]))
        copies.append(pltpu.make_async_copy(mixed_v, mixed_vv, sems.at[3]))
    copies.append(pltpu.make_async_copy(left_in, left, sems.at[1]))
    for copy in copies:
        copy.start()
    blocks = now.shape[0]
    me = place[0]
    if second:
        (alpha, beta, alpha2, beta2), (own, low, up) = pair_coefficients(
            gathered[...], count, False, (me, me - 1, me + 1)
        )
        acc_out[...] = record(record(acc[...], 0, alpha, beta), 1, alpha2, beta2)
        inv1 = 1.0 / beta[:, :1]
        beta2 = beta2[:, :1]
        inv = inv1 / beta2
        dev, gt, gv = own
    else:
        start_sq = jnp.sum(read_rows(gathered, 0), axis=0, keepdims=True)
        inv = jnp.sqrt(count / start_sq)[:, :1]
    for q in range(blocks):
        if second:
            old[q] = (held[q] + dev * before[q]) * inv1
            vec[q] = (resid[q] + gt * held[q] + gv * before[q]) * inv
        else:
            vec[q] = start[q] * inv
    for copy in copies[:-1]:
        copy.wait()
    small = []
    for slot, who, src, k, q in NEAR:
        block = (lower, upper)[who][src * side : (src + 1) * side, :]
        mixed = dot_nt(block, right[k, q])
        if second:
            _, near_t, near_v = (low, up)[who]
            mixed = mixed + near_t * mixed_tt[slot] + near_v * mixed_vv[slot]
        mixed = mixed * inv
        if not second:
            mixes[slot] = mixed
        small.append(mixed.astype(BF16))
    if not second:
        keep_mixes = pltpu.make_async_copy(mixes, mixes_out, sems.at[2])
        keep_mixes.start()
    copies[-1].wait()
    zero = jnp.zeros((1, 1), F32)
    corr, norm, image_dot = zero, zero, zero
    for q in range(blocks):
        v = vec[q]
        mask = cell_mask(dims, q, side)
        part_low = jnp.where(mask, from_lower(left, small, q), 0.0)
        part_up = jnp.where(mask, from_upper(left, small, q), 0.0)
        low_part[q] = part_low
        up_part[q] = part_up
        w = jnp.where(mask, from_own(left, right, v.astype(BF16), q), 0.0) + part_low + part_up
        corr = corr + total(v * w)
        norm = norm + total(v * v)
        if second:
            w = w - beta2 * old[q]
            image_dot = image_dot + total(v * w)
        now[q] = w
    near = ratio(image_dot if second else corr, norm)
    square, cross, uv, ut, uu = zero, zero, zero, zero, zero
    for q in range(blocks):
        t = now[q] - near * vec[q]
        now[q] = t
        sent[q * side : (q + 1) * side, :] = t.astype(BF16)
        square = square + total(t * t)
        cross = cross + total(t * vec[q])
        if second:
            u = old[q]
            uv = uv + total(u * vec[q])
            ut = ut + total(u * t)
            uu = uu + total(u * u)
    tail = jnp.zeros((16, side), F32)
    row = lax.broadcasted_iota(jnp.int32, tail.shape, 0)
    for k, part in enumerate(three_parts(near)):
        tail = jnp.where(row == k, part.astype(F32), tail)
    sent[blocks * side :, :] = tail.astype(BF16)
    values = {D: corr, S: square, V: norm, A: near, C: cross}
    if second:
        values.update({UV: uv, UT: ut, UU: uu, BETA: beta2})
    own_sums[...] = lay_rows(values, own_sums.shape)
    if not second:
        keep_mixes.wait()


def second_kernel(second, side, dims, left_in, right_in, lower, upper, own_sums, held, vec, low_part, up_part, *rest):
    if second:
        old, resid, sums, left, right, sems = rest
    else:
        sent, resid, sums, mixes_out, left, right, mixes, sems = rest
    copies = [
        pltpu.make_async_copy(right_in, right, sems.at[0]),
        pltpu.make_async_copy(left_in, left, sems.at[1]),
    ]
    for copy in copies:
        copy.start()
    blocks = held.shape[0]
    tails = [
        jnp.sum(x[blocks * side :, :].astype(F32)[:8], axis=0, keepdims=True)[:, :1]
        for x in (lower, upper)
    ]
    got = own_sums[0:1, :]
    near, norm, square = got[:, A : A + 1], got[:, V : V + 1], got[:, S : S + 1]
    low_dev, up_dev = tails[0] - near, tails[1] - near
    copies[0].wait()
    small = []
    for slot, who, src, k, q in NEAR:
        mixed = dot_nt((lower, upper)[who][src * side : (src + 1) * side, :], right[k, q])
        if not second:
            mixes[slot] = mixed
        small.append(mixed.astype(BF16))
    if not second:
        keep_mixes = pltpu.make_async_copy(mixes, mixes_out, sems.at[2])
        keep_mixes.start()
    copies[1].wait()
    zero = jnp.zeros((1, 1), F32)
    along_v, along_t = zero, zero
    for q in range(blocks):
        y = from_own(left, right, held[q].astype(BF16), q)
        y = y + from_lower(left, small, q) + from_upper(left, small, q)
        y = jnp.where(cell_mask(dims, q, side), y, 0.0)
        y = y + low_dev * low_part[q] + up_dev * up_part[q]
        resid[q] = y
        along_v = along_v + total(y * vec[q])
    pv = ratio(along_v, norm)
    for q in range(blocks):
        y = resid[q] - pv * vec[q]
        resid[q] = y
        along_t = along_t + total(y * held[q])
    pt = ratio(along_t, square)
    ee, ev, et, eu = zero, zero, zero, zero
    for q in range(blocks):
        e = resid[q] - pt * held[q]
        resid[q] = e
        if not second:
            sent[q * side : (q + 1) * side, :] = e.astype(BF16)
        ee = ee + total(e * e)
        ev = ev + total(e * vec[q])
        et = et + total(e * held[q])
        if second:
            eu = eu + total(e * old[q])
    values = {k: got[:, k : k + 1] for k in (D, S, V, A, C)}
    values.update({PV: pv, PT: pt, EE: ee, EV: ev, ET: et})
    if second:
        values.update({k: got[:, k : k + 1] for k in (UV, UT, UU, BETA)})
        values[EU] = eu
    sums[...] = lay_rows(values, sums.shape)
    if not second:
        keep_mixes.wait()


def dot_hp(a, b, dims):
    return lax.dot_general(a, b, (dims, ((), ())), precision=lax.Precision.HIGHEST, preferred_element_type=F32)

def panel_inverse(blocks, b):
    lane = lax.broadcasted_iota(jnp.int32, (8, 128), 1)
    row = lax.broadcasted_iota(jnp.int32, (8, 128), 0)
    first = lane < 64
    tiles = b // 8
    def column(k, r):
        one, two = (jnp.broadcast_to(x[8*r:8*r+8, k:k+1], (8, 128)) for x in blocks)
        return jnp.where(first, one, two)
    cols = [[column(k, r) for r in range(tiles)] for k in range(b)]
    own = jnp.where(first, lane, lane - 64)
    inv = [jnp.where(own == row + 8 * r, 1.0, 0.0).astype(F32) for r in range(tiles)]
    diag = [jnp.ones((8, 128), F32) for r in range(tiles)]
    for j in range(b):
        t, s = divmod(j, 8)
        pivot = jnp.broadcast_to(cols[j][t][s:s+1], (8, 128))
        diag[t] = jnp.where(row == s, pivot, diag[t])
        over = 1.0 / pivot
        inv_row = jnp.broadcast_to(inv[t][s:s+1], (8, 128))
        rows = [jnp.broadcast_to(cols[k][t][s:s+1], (8, 128)) for k in range(j + 1, b)]
        for r in range((j + 1) // 8, tiles):
            m = cols[j][r] * over
            if r == t:
                m = jnp.where(row > s, m, 0.0)
            for k in range(j + 1, b):
                cols[k][r] = cols[k][r] - m * rows[k - j - 1]
            inv[r] = inv[r] - m * inv_row
    full = jnp.concatenate([inv[r] * lax.rsqrt(diag[r]) for r in range(tiles)], axis=0)
    return full[:, :b], full[:, 64:64 + b]

def inverse_factors(work, b):
    n = work.shape[1]
    lane = lax.broadcasted_iota(jnp.int32, (b, n), 1)
    row = lax.broadcasted_iota(jnp.int32, (b, n), 0)
    for lo in range(0, n, b):
        hi = lo + b
        inv = panel_inverse([work[q, lo:hi, lo:hi] for q in range(2)], b)
        inside = jnp.logical_and(lane >= lo, lane < hi)
        unit = jnp.where(lane == row + lo, 1.0, 0.0)
        for q in range(2):
            panel = jnp.where(inside, unit, work[q, lo:hi, :])
            panel = dot_hp(inv[q], panel, ((1,), (0,)))
            work[q, lo:hi, :] = panel
            if hi < n:
                rest = work[q, hi:n, :]
                tail_lane = lax.broadcasted_iota(jnp.int32, rest.shape, 1)
                rest = jnp.where(jnp.logical_and(tail_lane >= lo, tail_lane < hi), 0.0, rest)
                work[q, hi:n, :] = rest - dot_hp(panel[:, hi:n], panel, ((0,), (0,)))

def truncate(ranks, sketch, vec, out, work, tall, rhs):
    n = sketch.shape[2]
    lane = lax.broadcasted_iota(jnp.int32, (1, n), 1)
    rows = lax.broadcasted_iota(jnp.int32, (n, n), 0)
    cols = lax.broadcasted_iota(jnp.int32, (n, n), 1)
    for q in range(2):
        y = dot_hp(vec[q], sketch[q], ((1,), (0,)))
        y = jnp.where(lane < ranks[q], y, 0.0)
        tall[q] = y
        spare = jnp.where(jnp.logical_and(rows == cols, cols >= ranks[q]), 1.0, 0.0)
        work[q] = dot_hp(y, y, ((0,), (0,))) + spare
    inverse_factors(work, PANEL)
    for q in range(2):
        rhs[q] = dot_hp(tall[q], vec[q], ((0,), (0,)))
        factor = jnp.where(rows >= cols, work[q], 0.0)
        inner = dot_hp(factor, rhs[q], ((1,), (0,)))
        coef = dot_hp(factor, inner, ((0,), (0,)))
        out[q] = dot_hp(tall[q], coef, ((1,), (0,)))


def finish_kernel(count, place, ranks, gathered, acc, resid, held, before, old, sketch, out, acc_out, vec, work, tall, rhs):
    (alpha, beta, alpha2, beta2), ((_, gt, gv, gu),) = pair_coefficients(
        gathered[...], count, True, (place[0],)
    )
    acc_out[...] = record(record(acc[...], 2, alpha, beta), 3, alpha2, beta2)
    inv = 1.0 / (beta * beta2)[:, :1]
    for q in range(held.shape[0]):
        vec[q] = (resid[q] + gt * held[q] + gv * before[q] + gu * old[q]) * inv
    truncate(ranks, sketch, vec, out, work, tall, rhs)


def keep(x):
    return pltpu.with_memory_space_constraint(x, pltpu.VMEM)


def shards(left_built, right_env, psi_init, block_dims, ranks, sketch):
    _, blocks, side, _ = psi_init.shape
    near = lax.axis_size("blk")
    count = float(near * blocks * side * side)
    secs = lax.axis_size("sec")
    left = lax.ppermute(left_built[0], "sec", [(i, (i + 1) % secs) for i in range(secs)])
    right = right_env[0]
    dims = block_dims[0]
    place = lax.axis_index("blk").astype(jnp.int32).reshape(1)
    block_f32 = jax.ShapeDtypeStruct((blocks, side, side), F32)
    flat = pltpu.VMEM((blocks * side, side), BF16)
    tailed = pltpu.VMEM((blocks * side + 16, side), BF16)
    rows = pltpu.VMEM((near, 128), F32)
    small = pltpu.VMEM((8, 128), F32)
    mixes = jax.ShapeDtypeStruct((6, side, side), F32)
    env = pltpu.VMEM(right.shape, BF16)
    mixes_here = pltpu.VMEM(mixes.shape, F32)

    def halo(block):
        low = lax.ppermute(block, "blk", [(i, i + 1) for i in range(near - 1)])
        up = lax.ppermute(block, "blk", [(i + 1, i) for i in range(near - 1)])
        return keep(low), keep(up)

    def everyone(sums):
        return keep(lax.all_to_all(sums, "blk", 0, 0, tiled=True))

    held, sent, sums = pl.pallas_call(
        begin_kernel,
        out_shape=(block_f32, flat, rows),
        in_specs=[SM, VM],
        out_specs=(VM, VM, VM),
        name="begin",
    )(dims, psi_init[0])
    low, up = halo(sent)
    acc = jnp.zeros((8, 128), F32)
    tailed_low, held, vec, low_part, up_part, own_sums, mixed_v = pl.pallas_call(
        functools.partial(first_kernel, False, count, side),
        out_shape=(tailed, block_f32, block_f32, block_f32, block_f32, small, mixes),
        in_specs=[SM, SM, VM, VM, AN, AN, VM, VM, VM],
        out_specs=(VM,) * 6 + (AN,),
        scratch_shapes=[env, env, mixes_here, pltpu.SemaphoreType.DMA((3,))],
        name="step0",
    )(place, dims, everyone(sums), acc, left, right, low, up, held)
    low, up = halo(tailed_low)
    sent, resid, sums, mixed_t = pl.pallas_call(
        functools.partial(second_kernel, False, side),
        out_shape=(flat, block_f32, rows, mixes),
        in_specs=[SM, AN, AN] + [VM] * 7,
        out_specs=(VM,) * 3 + (AN,),
        scratch_shapes=[env, env, mixes_here, pltpu.SemaphoreType.DMA((3,))],
        name="step1",
    )(dims, left, right, low, up, own_sums, held, vec, low_part, up_part)
    low, up = halo(sent)
    tailed_low, held, vec, low_part, up_part, own_sums, acc, old = pl.pallas_call(
        functools.partial(first_kernel, True, count, side),
        out_shape=(tailed,) + (block_f32,) * 4 + (small, small, block_f32),
        in_specs=[SM, SM, VM, VM, AN, AN] + [VM] * 5 + [AN, AN],
        out_specs=(VM,) * 8,
        scratch_shapes=[env, env, mixes_here, mixes_here, mixes_here, pltpu.SemaphoreType.DMA((4,))],
        name="step2",
    )(place, dims, everyone(sums), acc, left, right, low, up, resid, held, vec, mixed_t, mixed_v)
    low, up = halo(tailed_low)
    resid, sums = pl.pallas_call(
        functools.partial(second_kernel, True, side),
        out_shape=(block_f32, rows),
        in_specs=[SM, AN, AN] + [VM] * 8,
        out_specs=(VM, VM),
        scratch_shapes=[env, env, pltpu.SemaphoreType.DMA((2,))],
        name="step3",
    )(dims, left, right, low, up, own_sums, held, vec, low_part, up_part, old)
    rmax = sketch.shape[3]
    truncated, acc = pl.pallas_call(
        functools.partial(finish_kernel, count),
        out_shape=(block_f32, small),
        in_specs=[SM, SM] + [VM] * 7,
        out_specs=(VM, VM),
        scratch_shapes=[
            pltpu.VMEM((blocks, side, side), F32),
            pltpu.VMEM((blocks, rmax, rmax), F32),
            pltpu.VMEM((blocks, side, rmax), F32),
            pltpu.VMEM((blocks, rmax, side), F32),
        ],
        name="finish",
    )(place, ranks[0], everyone(sums), acc, resid, held, vec, old, sketch[0])
    return (truncated[None], acc[0:1, :STEPS], acc[1:2, :STEPS])


def solution(mesh):
    placed = (
        P("sec", None, "blk", None, None),
        P("sec", None, "blk", None, None),
        P("sec", "blk", None, None),
        P("sec", "blk"),
        P("sec", "blk"),
        P("sec", "blk", None, None),
    )
    return jax.shard_map(
        shards,
        mesh=mesh,
        in_specs=placed,
        out_specs=(P("sec", "blk", None, None), P("sec", None), P("sec", None)),
        check_vma=False,
    )
```

```python
import functools

import jax
import jax.numpy as jnp
from jax import lax
from jax.experimental import pallas as pl
from jax.experimental.pallas import tpu as pltpu
from jax.sharding import PartitionSpec as P

STEPS = 4
PANEL = 32
F32 = jnp.float32
BF16 = jnp.bfloat16
VM = pl.BlockSpec(memory_space=pltpu.VMEM)
SM = pl.BlockSpec(memory_space=pltpu.SMEM)
AN = pl.BlockSpec(memory_space=pl.ANY)


def total(x):
    return jnp.sum(jnp.sum(x, axis=0, keepdims=True), axis=1, keepdims=True)


def fold(x):
    return jnp.sum(x.reshape(x.shape[0] // 8, 8, x.shape[1]), axis=0)


def dot_nt(a, b):
    return lax.dot_general(a, b, (((1,), (1,)), ((), ())), preferred_element_type=F32)


def dot_nn(a, b):
    return jnp.dot(a, b, preferred_element_type=F32)


def cell_mask(dims, q, side):
    rows = lax.broadcasted_iota(jnp.int32, (side, side), 0)
    cols = lax.broadcasted_iota(jnp.int32, (side, side), 1)
    return jnp.logical_and(rows < dims[q], cols < dims[q])


def lay_rows(values, shape):
    lane = lax.broadcasted_iota(jnp.int32, shape, 1)
    out = jnp.zeros(shape, F32)
    for k, value in values.items():
        out = jnp.where(lane == k, value, out)
    return out


def read_rows(gathered, k):
    return jnp.broadcast_to(gathered[:, k : k + 1], gathered.shape)


D, S, V, A, C, PV, PT, EE, EV, ET, UV, UT, UU, EU, BETA = range(15)


def pair_coefficients(gathered, count, second, places):
    get = lambda k: read_rows(gathered, k)
    over = lambda x: jnp.sum(x, axis=0, keepdims=True)
    tt, vv, near, tv = get(S), get(V), get(A), get(C)
    pv, pt, ev, et = get(PV), get(PT), get(EV), get(ET)
    alpha = over(get(D)) / count
    dev = near - alpha
    resid = jnp.maximum(over(tt + 2.0 * dev * tv + dev * vv * dev), 0.0)
    beta = jnp.sqrt(resid / count + 1e-06)
    qt, qv = pt + dev, pv + dev * near
    inner = et + qt * tt + qv * tv + dev * (ev + qt * tv + qv * vv)
    if second:
        uv, ut, uu, eu = get(UV), get(UT), get(UU), get(EU)
        gu = dev * get(BETA)
        inner = inner + gu * ut + dev * (gu * uv)
    beta_sq = beta * beta
    alpha2 = over(inner) / (beta_sq * count)
    gt = qt - alpha2
    gv = qv - alpha2 * dev - beta_sq
    parts = get(EE) + gt * tt * gt + gv * vv * gv + 2.0 * (gt * et + gv * ev + gv * gt * tv)
    if second:
        parts = parts + gu * uu * gu + 2.0 * gu * (eu + gt * ut + gv * uv)
    resid2 = jnp.maximum(over(parts), 0.0)
    beta2 = jnp.sqrt(resid2 / (beta_sq * count) + 1e-06)
    row = lax.broadcasted_iota(jnp.int32, gathered.shape, 0)
    weights = [dev, gt, gv] + ([gu] if second else [])
    found = [
        [over(jnp.where(row == place, x, 0.0))[:, :1] for x in weights] for place in places
    ]
    return (alpha, beta, alpha2, beta2), found


def record(acc, step, alpha, beta):
    lane = lax.broadcasted_iota(jnp.int32, acc.shape, 1)
    row = lax.broadcasted_iota(jnp.int32, acc.shape, 0)
    here = lane == step
    acc = jnp.where(jnp.logical_and(here, row == 0), alpha, acc)
    return jnp.where(jnp.logical_and(here, row == 1), beta, acc)


def begin_kernel(dims, psi, masked, sent, sums):
    blocks, side = psi.shape[0], psi.shape[1]
    square = jnp.zeros((1, 1), F32)
    for q in range(blocks):
        x = jnp.where(cell_mask(dims, q, side), psi[q], 0.0)
        masked[q] = x
        sent[q * side : (q + 1) * side, :] = x.astype(BF16)
        square = square + total(x * x)
    sums[...] = jnp.broadcast_to(square, sums.shape)


NEAR = (
    (0, 0, 0, 2, 0),
    (1, 0, 1, 2, 1),
    (2, 1, 0, 3, 0),
    (3, 1, 1, 3, 1),
    (4, 0, 0, 4, 1),
    (5, 1, 1, 5, 0),
)


def from_lower(left, mixed, q):
    part = dot_nn(left[2, q], mixed[q])
    return part + dot_nn(left[4, q], mixed[4]) if q == 1 else part


def from_upper(left, mixed, q):
    part = dot_nn(left[3, q], mixed[2 + q])
    return part + dot_nn(left[5, q], mixed[5]) if q == 0 else part


def from_own(left, right, x, q):
    one = dot_nn(left[0, q], dot_nt(x, right[0, q]).astype(BF16))
    return one + dot_nn(left[1, q], dot_nt(x, right[1, q]).astype(BF16))


class Copies:
    def __init__(self, sems):
        self.sems, self.made = sems, {}

    def start(self, name, source, target):
        copy = pltpu.make_async_copy(source, target, self.sems.at[len(self.made)])
        self.made[name] = copy
        copy.start()

    def wait(self, *names):
        for name in names:
            self.made[name].wait()


def ratio(top, bottom):
    return jnp.where(bottom > 1e-12, top / jnp.maximum(bottom, 1e-12), 0.0)


def three_parts(x):
    high = x.astype(BF16)
    rest = x - high.astype(F32)
    middle = rest.astype(BF16)
    return high, middle, (rest - middle.astype(F32)).astype(BF16)


def own_kernel(side, dims, left_in, right_in, block, out, left, right, sems):
    copies = Copies(sems)
    copies.start("right", right_in.at[pl.ds(0, 2)], right)
    copies.start("left", left_in.at[pl.ds(0, 2)], left)
    copies.wait("right", "left")
    for q in range(out.shape[0]):
        part = from_own(left, right, block[q * side : (q + 1) * side, :], q)
        out[q] = jnp.where(cell_mask(dims, q, side), part, 0.0)


def first_kernel(second, count, side, place, dims, gathered, acc, lower, upper, left_in, right_in, *rest):
    if second:
        ins = dict(zip(("mt", "mv", "e", "t", "v", "oe", "ot", "ov"), rest[:8]))
        sent, own_sums, acc_out, now_out, vec_out, low_out, up_out, old_out = rest[8:16]
        now, vec, low_part, up_part, old = rest[16:21]
        left, right, sems = rest[21:24]
        here = dict(zip(ins, rest[24:]))
    else:
        ins = {"x": rest[0]}
        sent, own_sums, now_out, vec_out, low_out, up_out, own_out, mixes_out = rest[1:9]
        now, vec, low_part, up_part, own_part, mixes = rest[9:15]
        left, right, sems = rest[15:18]
        here = {"x": rest[18]}
    copies = Copies(sems)
    copies.start("right", right_in, right)
    for name, source in ins.items():
        copies.start(name, source, here[name])
    copies.start("left", left_in, left)
    blocks = now.shape[0]
    me = place[0]
    if second:
        (alpha, beta, alpha2, beta2), (own, low, up) = pair_coefficients(
            gathered[...], count, False, (me, me - 1, me + 1)
        )
        acc_out[...] = record(record(acc[...], 0, alpha, beta), 1, alpha2, beta2)
        inv1 = 1.0 / beta[:, :1]
        beta2 = beta2[:, :1]
        inv = inv1 / beta2
        dev, gt, gv = own
        copies.wait("right", "mt", "mv")
    else:
        start_sq = jnp.sum(read_rows(gathered, 0), axis=0, keepdims=True)
        inv = jnp.sqrt(count / start_sq)[:, :1]
        copies.wait("right")
    small = []
    for slot, who, src, k, q in NEAR:
        block = (lower, upper)[who][src * side : (src + 1) * side, :]
        mixed = dot_nt(block, right[k, q])
        if second:
            _, near_t, near_v = (low, up)[who]
            mixed = mixed + near_t * here["mt"][slot] + near_v * here["mv"][slot]
        mixed = mixed * inv
        if not second:
            mixes[slot] = mixed
        small.append(mixed.astype(BF16))
    if not second:
        copies.start("mixes", mixes, mixes_out)
    copies.wait(*ins) if not second else copies.wait("e", "t", "v", "oe", "ot", "ov")
    for q in range(blocks):
        if second:
            e, t, v = here["e"][q], here["t"][q], here["v"][q]
            old[q] = (t + dev * v) * inv1
            vec[q] = (e + gt * t + gv * v) * inv
        else:
            vec[q] = here["x"][q] * inv
        copies.start(("vec", q), vec.at[q], vec_out.at[q])
        if second:
            copies.start(("old", q), old.at[q], old_out.at[q])
    copies.wait("left")
    zero = jnp.zeros((8, side), F32)
    corr, norm, uv, uu = zero, zero, zero, zero
    for q in range(blocks):
        v = vec[q]
        mask = cell_mask(dims, q, side)
        part_low = jnp.where(mask, from_lower(left, small, q), 0.0)
        low_part[q] = part_low
        copies.start(("low", q), low_part.at[q], low_out.at[q])
        part_up = jnp.where(mask, from_upper(left, small, q), 0.0)
        up_part[q] = part_up
        copies.start(("up", q), up_part.at[q], up_out.at[q])
        if second:
            part = (here["oe"][q] + gt * here["ot"][q] + gv * here["ov"][q]) * inv
        else:
            part = jnp.where(mask, from_own(left, right, v.astype(BF16), q), 0.0)
            own_part[q] = part
            copies.start(("own", q), own_part.at[q], own_out.at[q])
        w = part + part_low + part_up
        corr = corr + fold(v * w)
        norm = norm + fold(v * v)
        if second:
            u = old[q]
            w = w - beta2 * u
            uv = uv + fold(u * v)
            uu = uu + fold(u * u)
        now[q] = w
    corr, norm = total(corr), total(norm)
    if second:
        uv, uu = total(uv), total(uu)
        near = ratio(corr - beta2 * uv, norm)
    else:
        near = ratio(corr, norm)
    tail = jnp.zeros((16, side), F32)
    row = lax.broadcasted_iota(jnp.int32, tail.shape, 0)
    for k, part in enumerate(three_parts(near)):
        tail = jnp.where(row == k, part.astype(F32), tail)
    sent[blocks * side :, :] = tail.astype(BF16)
    square, cross, ut = zero, zero, zero
    for q in range(blocks):
        t = now[q] - near * vec[q]
        now[q] = t
        copies.start(("now", q), now.at[q], now_out.at[q])
        sent[q * side : (q + 1) * side, :] = t.astype(BF16)
        square = square + fold(t * t)
        cross = cross + fold(t * vec[q])
        if second:
            ut = ut + fold(old[q] * t)
    values = {D: corr, S: total(square), V: norm, A: near, C: total(cross)}
    if second:
        values.update({UV: uv, UT: total(ut), UU: uu, BETA: beta2})
    own_sums[...] = lay_rows(values, own_sums.shape)
    names = ("vec", "low", "up", "now") + (("old",) if second else ("own",))
    copies.wait(*((name, q) for name in names for q in range(blocks)))
    if not second:
        copies.wait("mixes")


def second_kernel(second, side, dims, lower, upper, own_sums, left_in, right_in, *rest):
    many = 6 if second else 5
    ins = dict(zip(("own", "t", "v", "low", "up", "u"), rest[:many]))
    rest = rest[many:]
    if second:
        sums, resid_out, resid, left, right, sems = rest[:6]
        rest = rest[6:]
    else:
        sent, sums, resid_out, mixes_out, resid, mixes, left, right, sems = rest[:9]
        rest = rest[9:]
    here = dict(zip(ins, rest))
    copies = Copies(sems)
    copies.start("right", right_in.at[pl.ds(2, 4)], right.at[pl.ds(2, 4)])
    copies.start("left", left_in.at[pl.ds(2, 4)], left.at[pl.ds(2, 4)])
    for name, source in ins.items():
        copies.start(name, source, here[name])
    blocks = resid.shape[0]
    tails = [
        jnp.sum(x[blocks * side :, :].astype(F32)[:8], axis=0, keepdims=True)[:, :1]
        for x in (lower, upper)
    ]
    got = own_sums[0:1, :]
    near, norm, square = got[:, A : A + 1], got[:, V : V + 1], got[:, S : S + 1]
    skew = got[:, C : C + 1]
    low_dev, up_dev = tails[0] - near, tails[1] - near
    copies.wait("right")
    small = []
    for slot, who, src, k, q in NEAR:
        mixed = dot_nt((lower, upper)[who][src * side : (src + 1) * side, :], right[k, q])
        if not second:
            mixes[slot] = mixed
        small.append(mixed.astype(BF16))
    if not second:
        copies.start("mixes", mixes, mixes_out)
    copies.wait("left", *ins)
    zero = jnp.zeros((8, side), F32)
    along_v, along_t = zero, zero
    for q in range(blocks):
        y = from_lower(left, small, q) + from_upper(left, small, q)
        y = jnp.where(cell_mask(dims, q, side), y, 0.0) + here["own"][q]
        y = y + low_dev * here["low"][q] + up_dev * here["up"][q]
        resid[q] = y
        along_v = along_v + fold(y * here["v"][q])
        along_t = along_t + fold(y * here["t"][q])
    pv = ratio(total(along_v), norm)
    pt = ratio(total(along_t) - pv * skew, square)
    ee, ev, et, eu = zero, zero, zero, zero
    for q in range(blocks):
        t, v = here["t"][q], here["v"][q]
        e = resid[q] - pv * v - pt * t
        resid[q] = e
        copies.start(("e", q), resid.at[q], resid_out.at[q])
        if not second:
            sent[q * side : (q + 1) * side, :] = e.astype(BF16)
        ee = ee + fold(e * e)
        ev = ev + fold(e * v)
        et = et + fold(e * t)
        if second:
            eu = eu + fold(e * here["u"][q])
    values = {k: got[:, k : k + 1] for k in (D, S, V, A, C)}
    values.update({PV: pv, PT: pt, EE: total(ee), EV: total(ev), ET: total(et)})
    if second:
        values.update({k: got[:, k : k + 1] for k in (UV, UT, UU, BETA)})
        values[EU] = total(eu)
    sums[...] = lay_rows(values, sums.shape)
    copies.wait(*(("e", q) for q in range(blocks)))
    if not second:
        copies.wait("mixes")


def dot_hp(a, b, dims):
    return lax.dot_general(a, b, (dims, ((), ())), precision=lax.Precision.HIGHEST, preferred_element_type=F32)

def panel_inverse(blocks, b):
    lane = lax.broadcasted_iota(jnp.int32, (8, 128), 1)
    row = lax.broadcasted_iota(jnp.int32, (8, 128), 0)
    first = lane < 64
    tiles = b // 8
    def column(k, r):
        one, two = (jnp.broadcast_to(x[8*r:8*r+8, k:k+1], (8, 128)) for x in blocks)
        return jnp.where(first, one, two)
    cols = [[column(k, r) for r in range(tiles)] for k in range(b)]
    own = jnp.where(first, lane, lane - 64)
    inv = [jnp.where(own == row + 8 * r, 1.0, 0.0).astype(F32) for r in range(tiles)]
    diag = [jnp.ones((8, 128), F32) for r in range(tiles)]
    for j in range(b):
        t, s = divmod(j, 8)
        pivot = jnp.broadcast_to(cols[j][t][s:s+1], (8, 128))
        diag[t] = jnp.where(row == s, pivot, diag[t])
        over = 1.0 / pivot
        inv_row = jnp.broadcast_to(inv[t][s:s+1], (8, 128))
        rows = [jnp.broadcast_to(cols[k][t][s:s+1], (8, 128)) for k in range(j + 1, b)]
        for r in range((j + 1) // 8, tiles):
            m = cols[j][r] * over
            if r == t:
                m = jnp.where(row > s, m, 0.0)
            for k in range(j + 1, b):
                cols[k][r] = cols[k][r] - m * rows[k - j - 1]
            inv[r] = inv[r] - m * inv_row
    full = jnp.concatenate([inv[r] * lax.rsqrt(diag[r]) for r in range(tiles)], axis=0)
    return full[:, :b], full[:, 64:64 + b]

def inverse_factors(work, b):
    n = work.shape[1]
    lane = lax.broadcasted_iota(jnp.int32, (b, n), 1)
    row = lax.broadcasted_iota(jnp.int32, (b, n), 0)
    for lo in range(0, n, b):
        hi = lo + b
        inv = panel_inverse([work[q, lo:hi, lo:hi] for q in range(2)], b)
        inside = jnp.logical_and(lane >= lo, lane < hi)
        unit = jnp.where(lane == row + lo, 1.0, 0.0)
        for q in range(2):
            panel = jnp.where(inside, unit, work[q, lo:hi, :])
            panel = dot_hp(inv[q], panel, ((1,), (0,)))
            work[q, lo:hi, :] = panel
            if hi < n:
                rest = work[q, hi:n, :]
                tail_lane = lax.broadcasted_iota(jnp.int32, rest.shape, 1)
                rest = jnp.where(jnp.logical_and(tail_lane >= lo, tail_lane < hi), 0.0, rest)
                work[q, hi:n, :] = rest - dot_hp(panel[:, hi:n], panel, ((0,), (0,)))

def truncate(ranks, sketch, vec, out, work, tall, rhs):
    n = sketch.shape[2]
    lane = lax.broadcasted_iota(jnp.int32, (1, n), 1)
    rows = lax.broadcasted_iota(jnp.int32, (n, n), 0)
    cols = lax.broadcasted_iota(jnp.int32, (n, n), 1)
    for q in range(2):
        y = dot_hp(vec[q], sketch[q], ((1,), (0,)))
        y = jnp.where(lane < ranks[q], y, 0.0)
        tall[q] = y
        spare = jnp.where(jnp.logical_and(rows == cols, cols >= ranks[q]), 1.0, 0.0)
        work[q] = dot_hp(y, y, ((0,), (0,))) + spare
    inverse_factors(work, PANEL)
    for q in range(2):
        rhs[q] = dot_hp(tall[q], vec[q], ((0,), (0,)))
        factor = jnp.where(rows >= cols, work[q], 0.0)
        inner = dot_hp(factor, rhs[q], ((1,), (0,)))
        coef = dot_hp(factor, inner, ((0,), (0,)))
        out[q] = dot_hp(tall[q], coef, ((1,), (0,)))


def finish_kernel(count, place, ranks, gathered, acc, resid, held, before, old, sketch, out, acc_out, vec, work, tall, rhs):
    (alpha, beta, alpha2, beta2), ((_, gt, gv, gu),) = pair_coefficients(
        gathered[...], count, True, (place[0],)
    )
    acc_out[...] = record(record(acc[...], 2, alpha, beta), 3, alpha2, beta2)
    inv = 1.0 / (beta * beta2)[:, :1]
    for q in range(held.shape[0]):
        vec[q] = (resid[q] + gt * held[q] + gv * before[q] + gu * old[q]) * inv
    truncate(ranks, sketch, vec, out, work, tall, rhs)


def keep(x):
    return pltpu.with_memory_space_constraint(x, pltpu.VMEM)


def shards(left_built, right_env, psi_init, block_dims, ranks, sketch):
    _, blocks, side, _ = psi_init.shape
    near = lax.axis_size("blk")
    count = float(near * blocks * side * side)
    secs = lax.axis_size("sec")
    left = lax.ppermute(left_built[0], "sec", [(i, (i + 1) % secs) for i in range(secs)])
    right = right_env[0]
    dims = block_dims[0]
    place = lax.axis_index("blk").astype(jnp.int32).reshape(1)
    block_f32 = jax.ShapeDtypeStruct((blocks, side, side), F32)
    flat = pltpu.VMEM((blocks * side, side), BF16)
    tailed = pltpu.VMEM((blocks * side + 16, side), BF16)
    rows = pltpu.VMEM((near, 128), F32)
    small = pltpu.VMEM((8, 128), F32)
    mixes = jax.ShapeDtypeStruct((6, side, side), F32)
    env = pltpu.VMEM(right.shape, BF16)
    mixes_here = pltpu.VMEM(mixes.shape, F32)

    def halo(block):
        low = lax.ppermute(block, "blk", [(i, i + 1) for i in range(near - 1)])
        up = lax.ppermute(block, "blk", [(i + 1, i) for i in range(near - 1)])
        return keep(low), keep(up)

    def everyone(sums):
        return keep(lax.all_to_all(sums, "blk", 0, 0, tiled=True))

    block_here = pltpu.VMEM((blocks, side, side), F32)
    pair = pltpu.VMEM((2,) + right.shape[1:], BF16)
    dma = pltpu.SemaphoreType.DMA

    def own(block, name):
        return pl.pallas_call(
            functools.partial(own_kernel, side),
            out_shape=block_f32,
            in_specs=[SM, AN, AN, VM],
            out_specs=VM,
            scratch_shapes=[pair, pair, dma((2,))],
            name=name,
        )(dims, left, right, block)

    held, sent, sums = pl.pallas_call(
        begin_kernel,
        out_shape=(block_f32, flat, rows),
        in_specs=[SM, VM],
        out_specs=(VM, VM, VM),
        name="begin",
    )(dims, psi_init[0])
    low, up = halo(sent)
    acc = jnp.zeros((8, 128), F32)
    sent, own_sums, held, vec, low_part, up_part, own_v, mixed_v = pl.pallas_call(
        functools.partial(first_kernel, False, count, side),
        out_shape=(tailed, small) + (block_f32,) * 5 + (mixes,),
        in_specs=[SM, SM] + [VM] * 4 + [AN] * 3,
        out_specs=(VM,) * 2 + (AN,) * 6,
        scratch_shapes=[block_here] * 5 + [mixes_here, env, env, dma((16,)), block_here],
        name="step0",
    )(place, dims, everyone(sums), acc, low, up, left, right, held)
    low, up = halo(sent)
    own_t = own(sent, "own1")
    sent, sums, resid, mixed_t = pl.pallas_call(
        functools.partial(second_kernel, False, side),
        out_shape=(flat, rows, block_f32, mixes),
        in_specs=[SM] + [VM] * 3 + [AN] * 7,
        out_specs=(VM,) * 2 + (AN,) * 2,
        scratch_shapes=[block_here, mixes_here, env, env, dma((10,))] + [block_here] * 5,
        name="step1",
    )(dims, low, up, keep(own_sums), left, right, own_t, held, vec, low_part, up_part)
    low, up = halo(sent)
    own_e = own(sent, "own2")
    sent, own_sums, acc, held, vec, low_part, up_part, old = pl.pallas_call(
        functools.partial(first_kernel, True, count, side),
        out_shape=(tailed, small, small) + (block_f32,) * 5,
        in_specs=[SM, SM] + [VM] * 4 + [AN] * 10,
        out_specs=(VM,) * 3 + (AN,) * 5,
        scratch_shapes=[block_here] * 5 + [env, env, dma((20,)), mixes_here, mixes_here]
        + [block_here] * 6,
        name="step2",
    )(place, dims, everyone(sums), acc, low, up, left, right, mixed_t, mixed_v, resid, held, vec, own_e, own_t, own_v)
    low, up = halo(sent)
    own_t = own(sent, "own3")
    sums, resid = pl.pallas_call(
        functools.partial(second_kernel, True, side),
        out_shape=(rows, block_f32),
        in_specs=[SM] + [VM] * 3 + [AN] * 8,
        out_specs=(VM, AN),
        scratch_shapes=[block_here, env, env, dma((10,))] + [block_here] * 6,
        name="step3",
    )(dims, low, up, keep(own_sums), left, right, own_t, held, vec, low_part, up_part, old)
    rmax = sketch.shape[3]
    truncated, acc = pl.pallas_call(
        functools.partial(finish_kernel, count),
        out_shape=(block_f32, small),
        in_specs=[SM, SM] + [VM] * 7,
        out_specs=(VM, VM),
        scratch_shapes=[
            pltpu.VMEM((blocks, side, side), F32),
            pltpu.VMEM((blocks, rmax, rmax), F32),
            pltpu.VMEM((blocks, side, rmax), F32),
            pltpu.VMEM((blocks, rmax, side), F32),
        ],
        name="finish",
    )(place, ranks[0], everyone(sums), keep(acc), resid, held, vec, old, sketch[0])
    return (truncated[None], acc[0:1, :STEPS], acc[1:2, :STEPS])


def solution(mesh):
    placed = (
        P("sec", None, "blk", None, None),
        P("sec", None, "blk", None, None),
        P("sec", "blk", None, None),
        P("sec", "blk"),
        P("sec", "blk"),
        P("sec", "blk", None, None),
    )
    return jax.shard_map(
        shards,
        mesh=mesh,
        in_specs=placed,
        out_specs=(P("sec", "blk", None, None), P("sec", None), P("sec", None)),
        check_vma=False,
    )
```

```python
import functools

import jax
import jax.numpy as jnp
from jax import lax
from jax.experimental import pallas as pl
from jax.experimental.pallas import tpu as pltpu
from jax.sharding import PartitionSpec as P

STEPS = 4
PANEL = 32
F32 = jnp.float32
BF16 = jnp.bfloat16
VM = pl.BlockSpec(memory_space=pltpu.VMEM)
SM = pl.BlockSpec(memory_space=pltpu.SMEM)
AN = pl.BlockSpec(memory_space=pl.ANY)


def total(x):
    return jnp.sum(jnp.sum(x, axis=0, keepdims=True), axis=1, keepdims=True)


def fold(x):
    return jnp.sum(x.reshape(x.shape[0] // 8, 8, x.shape[1]), axis=0)


def dot_nt(a, b):
    return lax.dot_general(a, b, (((1,), (1,)), ((), ())), preferred_element_type=F32)


def dot_nn(a, b):
    return jnp.dot(a, b, preferred_element_type=F32)


def cell_mask(dims, q, side):
    rows = lax.broadcasted_iota(jnp.int32, (side, side), 0)
    cols = lax.broadcasted_iota(jnp.int32, (side, side), 1)
    return jnp.logical_and(rows < dims[q], cols < dims[q])


def lay_rows(values, shape):
    lane = lax.broadcasted_iota(jnp.int32, shape, 1)
    out = jnp.zeros(shape, F32)
    for k, value in values.items():
        out = jnp.where(lane == k, value, out)
    return out


def read_rows(gathered, k):
    return jnp.broadcast_to(gathered[:, k : k + 1], gathered.shape)


D, S, V, A, C, PV, PT, EE, EV, ET, UV, UT, UU, EU, BETA = range(15)


def pair_coefficients(gathered, count, second, places):
    get = lambda k: read_rows(gathered, k)
    over = lambda x: jnp.sum(x, axis=0, keepdims=True)
    tt, vv, near, tv = get(S), get(V), get(A), get(C)
    pv, pt, ev, et = get(PV), get(PT), get(EV), get(ET)
    alpha = over(get(D)) / count
    dev = near - alpha
    resid = jnp.maximum(over(tt + 2.0 * dev * tv + dev * vv * dev), 0.0)
    beta = jnp.sqrt(resid / count + 1e-06)
    qt, qv = pt + dev, pv + dev * near
    inner = et + qt * tt + qv * tv + dev * (ev + qt * tv + qv * vv)
    if second:
        uv, ut, uu, eu = get(UV), get(UT), get(UU), get(EU)
        gu = dev * get(BETA)
        inner = inner + gu * ut + dev * (gu * uv)
    beta_sq = beta * beta
    alpha2 = over(inner) / (beta_sq * count)
    gt = qt - alpha2
    gv = qv - alpha2 * dev - beta_sq
    parts = get(EE) + gt * tt * gt + gv * vv * gv + 2.0 * (gt * et + gv * ev + gv * gt * tv)
    if second:
        parts = parts + gu * uu * gu + 2.0 * gu * (eu + gt * ut + gv * uv)
    resid2 = jnp.maximum(over(parts), 0.0)
    beta2 = jnp.sqrt(resid2 / (beta_sq * count) + 1e-06)
    row = lax.broadcasted_iota(jnp.int32, gathered.shape, 0)
    weights = [dev, gt, gv] + ([gu] if second else [])
    found = [
        [over(jnp.where(row == place, x, 0.0))[:, :1] for x in weights] for place in places
    ]
    return (alpha, beta, alpha2, beta2), found


def record(acc, step, alpha, beta):
    lane = lax.broadcasted_iota(jnp.int32, acc.shape, 1)
    row = lax.broadcasted_iota(jnp.int32, acc.shape, 0)
    here = lane == step
    acc = jnp.where(jnp.logical_and(here, row == 0), alpha, acc)
    return jnp.where(jnp.logical_and(here, row == 1), beta, acc)


def begin_kernel(dims, psi, masked, sums):
    blocks, side = psi.shape[0], psi.shape[1]
    square = jnp.zeros((1, 1), F32)
    for q in range(blocks):
        x = jnp.where(cell_mask(dims, q, side), psi[q], 0.0)
        masked[q] = x
        square = square + total(x * x)
    sums[...] = jnp.broadcast_to(square, sums.shape)


def scale_kernel(count, gathered, masked, vec, sent):
    start_sq = jnp.sum(read_rows(gathered, 0), axis=0, keepdims=True)
    scale = jnp.sqrt(count / start_sq)[:, :1]
    blocks, side = vec.shape[0], vec.shape[1]
    for q in range(blocks):
        v = masked[q] * scale
        vec[q] = v
        sent[q * side : (q + 1) * side, :] = v.astype(BF16)


NEAR = (
    (0, 0, 0, 2, 0),
    (1, 0, 1, 2, 1),
    (2, 1, 0, 3, 0),
    (3, 1, 1, 3, 1),
    (4, 0, 0, 4, 1),
    (5, 1, 1, 5, 0),
)


def parts_of(mixed, fine):
    high = mixed.astype(BF16)
    return (high, (mixed - high.astype(F32)).astype(BF16)) if fine else (high,)


def times(left, parts):
    return sum(dot_nn(left, part) for part in parts[1:]) + dot_nn(left, parts[0])


def from_lower(left, mixed, q):
    part = times(left[2, q], mixed[q])
    return part + times(left[4, q], mixed[4]) if q == 1 else part


def from_upper(left, mixed, q):
    part = times(left[3, q], mixed[2 + q])
    return part + times(left[5, q], mixed[5]) if q == 0 else part


def from_own(left, right, x, q, fine):
    one = times(left[0, q], parts_of(dot_nt(x, right[0, q]), fine))
    return one + times(left[1, q], parts_of(dot_nt(x, right[1, q]), fine))


class Copies:
    def __init__(self, sems):
        self.sems, self.made = sems, {}

    def start(self, name, source, target):
        copy = pltpu.make_async_copy(source, target, self.sems.at[len(self.made)])
        self.made[name] = copy
        copy.start()

    def wait(self, *names):
        for name in names:
            self.made[name].wait()


def ratio(top, bottom):
    return jnp.where(bottom > 1e-12, top / jnp.maximum(bottom, 1e-12), 0.0)


def three_parts(x):
    high = x.astype(BF16)
    rest = x - high.astype(F32)
    middle = rest.astype(BF16)
    return high, middle, (rest - middle.astype(F32)).astype(BF16)


def own_kernel(side, dims, left_in, right_in, block, out, left, right, sems):
    copies = Copies(sems)
    copies.start("right", right_in.at[pl.ds(0, 2)], right)
    copies.start("left", left_in.at[pl.ds(0, 2)], left)
    copies.wait("right", "left")
    for q in range(out.shape[0]):
        part = from_own(left, right, block[q * side : (q + 1) * side, :], q, True)
        out[q] = jnp.where(cell_mask(dims, q, side), part, 0.0)


def first_kernel(second, count, side, place, dims, gathered, lower, upper, left_in, right_in, *rest):
    if second:
        ins = dict(zip(("mt", "mv", "e", "t", "v", "oe", "ot", "ov"), rest[:8]))
        sent, own_sums, acc_out, now_out, vec_out, low_out, up_out, old_out = rest[8:16]
        now, vec, low_part, up_part, old = rest[16:21]
        left, right, sems = rest[21:24]
        here = dict(zip(ins, rest[24:]))
    else:
        ins = {"x": rest[0]}
        sent, own_sums, now_out, vec_out, low_out, up_out, own_out, mixes_out = rest[1:9]
        now, vec, low_part, up_part, own_part, mixes = rest[9:15]
        left, right, sems = rest[15:18]
        here = {"x": rest[18]}
    copies = Copies(sems)
    copies.start("right", right_in, right)
    for name, source in ins.items():
        copies.start(name, source, here[name])
    copies.start("left", left_in, left)
    blocks = now.shape[0]
    me = place[0]
    if second:
        (alpha, beta, alpha2, beta2), (own, low, up) = pair_coefficients(
            gathered[...], count, False, (me, me - 1, me + 1)
        )
        blank = jnp.zeros(acc_out.shape, F32)
        acc_out[...] = record(record(blank, 0, alpha, beta), 1, alpha2, beta2)
        inv1 = 1.0 / beta[:, :1]
        beta2 = beta2[:, :1]
        inv = inv1 / beta2
        dev, gt, gv = own
        copies.wait("right", "mt", "mv")
    else:
        copies.wait("right")
    small = []
    for slot, who, src, k, q in NEAR:
        block = (lower, upper)[who][src * side : (src + 1) * side, :]
        mixed = dot_nt(block, right[k, q])
        if second:
            _, near_t, near_v = (low, up)[who]
            mixed = mixed + near_t * here["mt"][slot] + near_v * here["mv"][slot]
            mixed = mixed * inv
        else:
            mixes[slot] = mixed
        small.append(parts_of(mixed, second))
    if not second:
        copies.start("mixes", mixes, mixes_out)
    copies.wait(*ins) if not second else copies.wait("e", "t", "v", "oe", "ot", "ov")
    for q in range(blocks):
        if second:
            e, t, v = here["e"][q], here["t"][q], here["v"][q]
            old[q] = (t + dev * v) * inv1
            vec[q] = (e + gt * t + gv * v) * inv
        else:
            vec[q] = here["x"][q]
        copies.start(("vec", q), vec.at[q], vec_out.at[q])
        if second:
            copies.start(("old", q), old.at[q], old_out.at[q])
    copies.wait("left")
    zero = jnp.zeros((8, side), F32)
    corr, norm, uv, uu = zero, zero, zero, zero
    for q in range(blocks):
        v = vec[q]
        mask = cell_mask(dims, q, side)
        part_low = jnp.where(mask, from_lower(left, small, q), 0.0)
        low_part[q] = part_low
        copies.start(("low", q), low_part.at[q], low_out.at[q])
        part_up = jnp.where(mask, from_upper(left, small, q), 0.0)
        up_part[q] = part_up
        copies.start(("up", q), up_part.at[q], up_out.at[q])
        if second:
            part = (here["oe"][q] + gt * here["ot"][q] + gv * here["ov"][q]) * inv
        else:
            part = jnp.where(mask, from_own(left, right, v.astype(BF16), q, False), 0.0)
            own_part[q] = part
            copies.start(("own", q), own_part.at[q], own_out.at[q])
        w = part + part_low + part_up
        corr = corr + fold(v * w)
        norm = norm + fold(v * v)
        if second:
            u = old[q]
            w = w - beta2 * u
            uv = uv + fold(u * v)
            uu = uu + fold(u * u)
        now[q] = w
    corr, norm = total(corr), total(norm)
    if second:
        uv, uu = total(uv), total(uu)
        near = ratio(corr - beta2 * uv, norm)
    else:
        near = ratio(corr, norm)
    tail = jnp.zeros((16, side), F32)
    row = lax.broadcasted_iota(jnp.int32, tail.shape, 0)
    for k, part in enumerate(three_parts(near)):
        tail = jnp.where(row == k, part.astype(F32), tail)
    sent[blocks * side :, :] = tail.astype(BF16)
    square, cross, ut = zero, zero, zero
    for q in range(blocks):
        t = now[q] - near * vec[q]
        now[q] = t
        copies.start(("now", q), now.at[q], now_out.at[q])
        sent[q * side : (q + 1) * side, :] = t.astype(BF16)
        square = square + fold(t * t)
        cross = cross + fold(t * vec[q])
        if second:
            ut = ut + fold(old[q] * t)
    values = {D: corr, S: total(square), V: norm, A: near, C: total(cross)}
    if second:
        values.update({UV: uv, UT: total(ut), UU: uu, BETA: beta2})
    own_sums[...] = lay_rows(values, own_sums.shape)
    names = ("vec", "low", "up", "now") + (("old",) if second else ("own",))
    copies.wait(*((name, q) for name in names for q in range(blocks)))
    if not second:
        copies.wait("mixes")


def second_kernel(second, side, dims, lower, upper, own_sums, left_in, right_in, *rest):
    many = 6 if second else 5
    ins = dict(zip(("own", "t", "v", "low", "up", "u"), rest[:many]))
    rest = rest[many:]
    if second:
        sums, resid_out, resid, left, right, sems = rest[:6]
        rest = rest[6:]
    else:
        sent, sums, resid_out, mixes_out, resid, mixes, left, right, sems = rest[:9]
        rest = rest[9:]
    here = dict(zip(ins, rest))
    copies = Copies(sems)
    copies.start("right", right_in.at[pl.ds(2, 4)], right.at[pl.ds(2, 4)])
    copies.start("left", left_in.at[pl.ds(2, 4)], left.at[pl.ds(2, 4)])
    for name, source in ins.items():
        copies.start(name, source, here[name])
    blocks = resid.shape[0]
    tails = [
        jnp.sum(x[blocks * side :, :].astype(F32)[:8], axis=0, keepdims=True)[:, :1]
        for x in (lower, upper)
    ]
    got = own_sums[0:1, :]
    near, norm, square = got[:, A : A + 1], got[:, V : V + 1], got[:, S : S + 1]
    skew = got[:, C : C + 1]
    low_dev, up_dev = tails[0] - near, tails[1] - near
    copies.wait("right")
    small = []
    for slot, who, src, k, q in NEAR:
        mixed = dot_nt((lower, upper)[who][src * side : (src + 1) * side, :], right[k, q])
        if not second:
            mixes[slot] = mixed
        small.append(parts_of(mixed, True))
    if not second:
        copies.start("mixes", mixes, mixes_out)
    copies.wait("left", *ins)
    zero = jnp.zeros((8, side), F32)
    along_v, along_t = zero, zero
    for q in range(blocks):
        y = from_lower(left, small, q) + from_upper(left, small, q)
        y = jnp.where(cell_mask(dims, q, side), y, 0.0) + here["own"][q]
        y = y + low_dev * here["low"][q] + up_dev * here["up"][q]
        resid[q] = y
        along_v = along_v + fold(y * here["v"][q])
        along_t = along_t + fold(y * here["t"][q])
    pv = ratio(total(along_v), norm)
    pt = ratio(total(along_t) - pv * skew, square)
    ee, ev, et, eu = zero, zero, zero, zero
    for q in range(blocks):
        t, v = here["t"][q], here["v"][q]
        e = resid[q] - pv * v - pt * t
        resid[q] = e
        copies.start(("e", q), resid.at[q], resid_out.at[q])
        if not second:
            sent[q * side : (q + 1) * side, :] = e.astype(BF16)
        ee = ee + fold(e * e)
        ev = ev + fold(e * v)
        et = et + fold(e * t)
        if second:
            eu = eu + fold(e * here["u"][q])
    values = {k: got[:, k : k + 1] for k in (D, S, V, A, C)}
    values.update({PV: pv, PT: pt, EE: total(ee), EV: total(ev), ET: total(et)})
    if second:
        values.update({k: got[:, k : k + 1] for k in (UV, UT, UU, BETA)})
        values[EU] = total(eu)
    sums[...] = lay_rows(values, sums.shape)
    copies.wait(*(("e", q) for q in range(blocks)))
    if not second:
        copies.wait("mixes")


def dot_hp(a, b, dims):
    return lax.dot_general(a, b, (dims, ((), ())), precision=lax.Precision.HIGHEST, preferred_element_type=F32)

def panel_inverse(blocks, b):
    lane = lax.broadcasted_iota(jnp.int32, (8, 128), 1)
    row = lax.broadcasted_iota(jnp.int32, (8, 128), 0)
    first = lane < 64
    tiles = b // 8
    def column(k, r):
        one, two = (jnp.broadcast_to(x[8*r:8*r+8, k:k+1], (8, 128)) for x in blocks)
        return jnp.where(first, one, two)
    cols = [[column(k, r) for r in range(tiles)] for k in range(b)]
    own = jnp.where(first, lane, lane - 64)
    inv = [jnp.where(own == row + 8 * r, 1.0, 0.0).astype(F32) for r in range(tiles)]
    diag = [jnp.ones((8, 128), F32) for r in range(tiles)]
    for j in range(b):
        t, s = divmod(j, 8)
        pivot = jnp.broadcast_to(cols[j][t][s:s+1], (8, 128))
        diag[t] = jnp.where(row == s, pivot, diag[t])
        over = 1.0 / pivot
        inv_row = jnp.broadcast_to(inv[t][s:s+1], (8, 128))
        rows = [jnp.broadcast_to(cols[k][t][s:s+1], (8, 128)) for k in range(j + 1, b)]
        for r in range((j + 1) // 8, tiles):
            m = cols[j][r] * over
            if r == t:
                m = jnp.where(row > s, m, 0.0)
            for k in range(j + 1, b):
                cols[k][r] = cols[k][r] - m * rows[k - j - 1]
            inv[r] = inv[r] - m * inv_row
    full = jnp.concatenate([inv[r] * lax.rsqrt(diag[r]) for r in range(tiles)], axis=0)
    return full[:, :b], full[:, 64:64 + b]

def inverse_factors(work, b):
    n = work.shape[1]
    lane = lax.broadcasted_iota(jnp.int32, (b, n), 1)
    row = lax.broadcasted_iota(jnp.int32, (b, n), 0)
    for lo in range(0, n, b):
        hi = lo + b
        inv = panel_inverse([work[q, lo:hi, lo:hi] for q in range(2)], b)
        inside = jnp.logical_and(lane >= lo, lane < hi)
        unit = jnp.where(lane == row + lo, 1.0, 0.0)
        for q in range(2):
            panel = jnp.where(inside, unit, work[q, lo:hi, :])
            panel = dot_hp(inv[q], panel, ((1,), (0,)))
            work[q, lo:hi, :] = panel
            if hi < n:
                rest = work[q, hi:n, :]
                tail_lane = lax.broadcasted_iota(jnp.int32, rest.shape, 1)
                rest = jnp.where(jnp.logical_and(tail_lane >= lo, tail_lane < hi), 0.0, rest)
                work[q, hi:n, :] = rest - dot_hp(panel[:, hi:n], panel, ((0,), (0,)))

def truncate(ranks, sketch, vec, out, work, tall, rhs):
    n = sketch.shape[2]
    lane = lax.broadcasted_iota(jnp.int32, (1, n), 1)
    rows = lax.broadcasted_iota(jnp.int32, (n, n), 0)
    cols = lax.broadcasted_iota(jnp.int32, (n, n), 1)
    for q in range(2):
        y = dot_hp(vec[q], sketch[q], ((1,), (0,)))
        y = jnp.where(lane < ranks[q], y, 0.0)
        tall[q] = y
        spare = jnp.where(jnp.logical_and(rows == cols, cols >= ranks[q]), 1.0, 0.0)
        work[q] = dot_hp(y, y, ((0,), (0,))) + spare
    inverse_factors(work, PANEL)
    for q in range(2):
        rhs[q] = dot_hp(tall[q], vec[q], ((0,), (0,)))
        factor = jnp.where(rows >= cols, work[q], 0.0)
        inner = dot_hp(factor, rhs[q], ((1,), (0,)))
        coef = dot_hp(factor, inner, ((0,), (0,)))
        out[q] = dot_hp(tall[q], coef, ((1,), (0,)))


def finish_kernel(count, place, ranks, gathered, acc, resid, held, before, old, sketch, out, acc_out, vec, work, tall, rhs):
    (alpha, beta, alpha2, beta2), ((_, gt, gv, gu),) = pair_coefficients(
        gathered[...], count, True, (place[0],)
    )
    acc_out[...] = record(record(acc[...], 2, alpha, beta), 3, alpha2, beta2)
    inv = 1.0 / (beta * beta2)[:, :1]
    for q in range(held.shape[0]):
        vec[q] = (resid[q] + gt * held[q] + gv * before[q] + gu * old[q]) * inv
    truncate(ranks, sketch, vec, out, work, tall, rhs)


def keep(x):
    return pltpu.with_memory_space_constraint(x, pltpu.VMEM)


def shards(left_built, right_env, psi_init, block_dims, ranks, sketch):
    _, blocks, side, _ = psi_init.shape
    near = lax.axis_size("blk")
    count = float(near * blocks * side * side)
    secs = lax.axis_size("sec")
    left = lax.ppermute(left_built[0], "sec", [(i, (i + 1) % secs) for i in range(secs)])
    right = right_env[0]
    dims = block_dims[0]
    place = lax.axis_index("blk").astype(jnp.int32).reshape(1)
    block_f32 = jax.ShapeDtypeStruct((blocks, side, side), F32)
    flat = pltpu.VMEM((blocks * side, side), BF16)
    tailed = pltpu.VMEM((blocks * side + 16, side), BF16)
    rows = pltpu.VMEM((near, 128), F32)
    small = pltpu.VMEM((8, 128), F32)
    mixes = jax.ShapeDtypeStruct((6, side, side), F32)
    env = pltpu.VMEM(right.shape, BF16)
    mixes_here = pltpu.VMEM(mixes.shape, F32)

    def halo(block):
        low = lax.ppermute(block, "blk", [(i, i + 1) for i in range(near - 1)])
        up = lax.ppermute(block, "blk", [(i + 1, i) for i in range(near - 1)])
        return keep(low), keep(up)

    def everyone(sums):
        return keep(lax.all_to_all(sums, "blk", 0, 0, tiled=True))

    block_here = pltpu.VMEM((blocks, side, side), F32)
    pair = pltpu.VMEM((2,) + right.shape[1:], BF16)
    dma = pltpu.SemaphoreType.DMA

    def own(block, name):
        return pl.pallas_call(
            functools.partial(own_kernel, side),
            out_shape=block_f32,
            in_specs=[SM, AN, AN, VM],
            out_specs=VM,
            scratch_shapes=[pair, pair, dma((2,))],
            name=name,
        )(dims, left, right, block)

    held, sums = pl.pallas_call(
        begin_kernel,
        out_shape=(pltpu.VMEM((blocks, side, side), F32), rows),
        in_specs=[SM, VM],
        out_specs=(VM, VM),
        name="begin",
    )(dims, psi_init[0])
    held, sent = pl.pallas_call(
        functools.partial(scale_kernel, count),
        out_shape=(block_f32, flat),
        in_specs=[VM, VM],
        out_specs=(VM, VM),
        name="scale",
    )(everyone(sums), keep(held))
    low, up = halo(sent)
    sent, own_sums, held, vec, low_part, up_part, own_v, mixed_v = pl.pallas_call(
        functools.partial(first_kernel, False, count, side),
        out_shape=(tailed, small) + (block_f32,) * 5 + (mixes,),
        in_specs=[SM, SM] + [VM] * 3 + [AN] * 3,
        out_specs=(VM,) * 2 + (AN,) * 6,
        scratch_shapes=[block_here] * 5 + [mixes_here, env, env, dma((16,)), block_here],
        name="step0",
    )(place, dims, keep(sums), low, up, left, right, held)
    low, up = halo(sent)
    own_t = own(sent, "own1")
    sent, sums, resid, mixed_t = pl.pallas_call(
        functools.partial(second_kernel, False, side),
        out_shape=(flat, rows, block_f32, mixes),
        in_specs=[SM] + [VM] * 3 + [AN] * 7,
        out_specs=(VM,) * 2 + (AN,) * 2,
        scratch_shapes=[block_here, mixes_here, env, env, dma((10,))] + [block_here] * 5,
        name="step1",
    )(dims, low, up, keep(own_sums), left, right, own_t, held, vec, low_part, up_part)
    low, up = halo(sent)
    own_e = own(sent, "own2")
    sent, own_sums, acc, held, vec, low_part, up_part, old = pl.pallas_call(
        functools.partial(first_kernel, True, count, side),
        out_shape=(tailed, small, small) + (block_f32,) * 5,
        in_specs=[SM, SM] + [VM] * 3 + [AN] * 10,
        out_specs=(VM,) * 3 + (AN,) * 5,
        scratch_shapes=[block_here] * 5 + [env, env, dma((20,)), mixes_here, mixes_here]
        + [block_here] * 6,
        name="step2",
    )(place, dims, everyone(sums), low, up, left, right, mixed_t, mixed_v, resid, held, vec, own_e, own_t, own_v)
    low, up = halo(sent)
    own_t = own(sent, "own3")
    sums, resid = pl.pallas_call(
        functools.partial(second_kernel, True, side),
        out_shape=(rows, block_f32),
        in_specs=[SM] + [VM] * 3 + [AN] * 8,
        out_specs=(VM, AN),
        scratch_shapes=[block_here, env, env, dma((10,))] + [block_here] * 6,
        name="step3",
    )(dims, low, up, keep(own_sums), left, right, own_t, held, vec, low_part, up_part, old)
    rmax = sketch.shape[3]
    truncated, acc = pl.pallas_call(
        functools.partial(finish_kernel, count),
        out_shape=(block_f32, small),
        in_specs=[SM, SM] + [VM] * 7,
        out_specs=(VM, VM),
        scratch_shapes=[
            pltpu.VMEM((blocks, side, side), F32),
            pltpu.VMEM((blocks, rmax, rmax), F32),
            pltpu.VMEM((blocks, side, rmax), F32),
            pltpu.VMEM((blocks, rmax, side), F32),
        ],
        name="finish",
    )(place, ranks[0], everyone(sums), keep(acc), resid, held, vec, old, sketch[0])
    return (truncated[None], acc[0:1, :STEPS], acc[1:2, :STEPS])


def solution(mesh):
    placed = (
        P("sec", None, "blk", None, None),
        P("sec", None, "blk", None, None),
        P("sec", "blk", None, None),
        P("sec", "blk"),
        P("sec", "blk"),
        P("sec", "blk", None, None),
    )
    return jax.shard_map(
        shards,
        mesh=mesh,
        in_specs=placed,
        out_specs=(P("sec", "blk", None, None), P("sec", None), P("sec", None)),
        check_vma=False,
    )
```
